32 devices in a mesh: parts: 2 (over x), chan: 4 (over y, core), tmpl: 4 (over z).
Axes of the slice: x: 2, y: 2, z: 4, core: 2. Of those that a mesh axis runs over, the one named last changes fastest.
Arguments:
- raw_traces: float32 [4096, 2816], P(('chan', 'tmpl'), 'parts'), parts along dimension 1, may hold values from -50 to 50
- filter_taps: float32 [129], replicated, may hold values from -0.5 to 0.5
- templates: bfloat16 [32, 200, 4096], P('tmpl', None, 'chan'), may hold values from -6 to 6
- offsets: int32 [32], P('tmpl'), may hold values from 0 to 56
- channel_mask: int32 [32, 4096], P('tmpl'), may hold values from 0 to 1, as said below
Outputs:
- detection: float32 [32, 2048], P('tmpl', ('parts', 'chan')), parts along dimension 1
The draws below stay inside these ranges and needn't reach their ends.
There are 2 independent parts, one for each index of `parts`. The reference program is written for one: setup_inputs(seed, part) draws one part's arguments, and reference() takes and returns one part's arrays. A program takes and returns all parts, laid end to end along the dimension named above; an argument that names none is the same for every part. Nothing has to cross between parts.
Inputs may be any that keep to these rules, and one draw needn't show every extreme that they name: `channel_mask`: each template uses one contiguous run of 4 or more blocks of 128 channels, starting and ending at multiples of 128; some template uses all channels.
All inputs are finite; a program needn't handle non-finite values.
Results may differ from the reference program's by a relative error of at most 0.004.
Values may be sent and summed in bfloat16 or wider, within the bound.
A program may use at most 128 MiB of HBM per device.

```python
import math
import jax
import jax.numpy as jnp
from jax import lax

CHANNELS = 4096
TMPL_LEN = 200
SPAN = 256
FIR_TAPS = 129
TEMPLATES = 32
LAGS = 1024
SAMPLES = 1408


def draw_raw_traces(key, part):
    key_gain, key_noise = jax.random.split(key, 2)
    gains = jnp.exp(jax.random.uniform(key_gain, (CHANNELS, 1), jnp.float32, 0.0, math.log(10.0)))
    noise = jnp.clip(jax.random.normal(key_noise, (CHANNELS, SAMPLES), jnp.float32), -5.0, 5.0)
    return (gains * noise).astype(jnp.float32)


def draw_channel_mask(key, part):
    key_span, key_first, key_full = jax.random.split(jax.random.fold_in(key, 7), 3)
    unit_width = CHANNELS // 32
    span_units = jax.random.randint(key_span, (TEMPLATES, 1), 4, 33)
    full_row = jax.random.randint(key_full, (), 0, TEMPLATES)
    rows_index = jnp.arange(TEMPLATES, dtype=jnp.int32)[:, None]
    span_units = jnp.where(rows_index == full_row, 32, span_units)
    first_unit = jax.random.randint(key_first, (TEMPLATES, 1), 0, 33 - span_units)
    columns = jnp.arange(CHANNELS, dtype=jnp.int32)[None, :] // unit_width
    inside = (columns >= first_unit) & (columns < first_unit + span_units)
    return inside.astype(jnp.int32)


def with_ends(entries, rng, least, largest):
    dims = entries.shape
    place = [jax.random.randint(jax.random.fold_in(rng, axis), (), 0, dims[axis]) for axis in range(len(dims))]
    entries = entries.at[tuple(place)].set(least)
    longest = dims.index(max(dims))
    place[longest] = (place[longest] + 1) % dims[longest]
    return entries.at[tuple(place)].set(largest)


def block_scale(stream_key, extent, shards, smallest, top_value):
    level = 1.0
    for position, blocks in shards:
        heights = jax.random.uniform(jax.random.fold_in(jax.random.fold_in(stream_key, 6), position), (blocks,), jnp.float32, smallest / len(shards), top_value / len(shards))
        level = level * jnp.repeat(jnp.exp(heights), extent[position] // blocks).reshape((-1,) + (1,) * (len(extent) - 1 - position))
    return level


def bell_draw(rng, extent, width, reach, shards=(), held_as=jnp.bfloat16):
    entries = jax.random.normal(rng, extent, jnp.float32) * width
    if len(shards) > 0:
        entries = block_scale(rng, extent, shards, -0.22, 0.18) * entries
    return jnp.clip(entries, min=-reach, max=reach).astype(held_as)


def setup_inputs(seed: int = 0, part: int = 0) -> dict:
    streams_of = jax.random.split(jax.random.key(seed), 6)
    part_keys = jax.random.split(jax.random.fold_in(streams_of[5], part), 6)
    return {
        "raw_traces": draw_raw_traces(jax.random.fold_in(jax.random.fold_in(streams_of[5], part), 71), part),
        "filter_taps": bell_draw(streams_of[1], (FIR_TAPS,), FIR_TAPS ** -0.5, 0.5, (), jnp.float32),
        "templates": bell_draw(streams_of[2], (TEMPLATES, TMPL_LEN, CHANNELS), 1.0, 6.0, ((0, 4), (2, 4))),
        "offsets": with_ends(jax.random.randint(streams_of[3], (TEMPLATES,), 0, SPAN - TMPL_LEN + 1), jax.random.fold_in(streams_of[3], 1), 0, SPAN - TMPL_LEN).astype(jnp.int32),
        "channel_mask": draw_channel_mask(jax.random.fold_in(streams_of[5], 71), part),
    }


def filter_traces(raw_traces, filter_taps):
    output = lax.conv_general_dilated(raw_traces[:, None, :], filter_taps[None, None, :], (1,), 'VALID', precision=lax.Precision.HIGHEST)
    return lax.optimization_barrier(output[:, 0, :].astype(jnp.bfloat16))

def shape_templates(templates, channel_mask):
    values = templates.astype(jnp.float32)
    rms_scale = jnp.sqrt(lax.optimization_barrier(jnp.mean(values * values, axis=1, keepdims=True)) + 1e-06)
    return (channel_mask.astype(jnp.float32)[:, None, :] * values / rms_scale).astype(jnp.bfloat16)

def skew_sum(product, count_out):
    height, length = product.shape
    flattened = jnp.concatenate([product.reshape(-1), jnp.zeros((height,), product.dtype)])
    return flattened.reshape(height, length + 1)[:, :count_out].sum(axis=0)

def window_energy(masses, offsets, count_out):

    def one_row(row_values, offset_value):
        return lax.dynamic_slice_in_dim(row_values, offset_value, count_out + TMPL_LEN - 1)
    segments = jax.vmap(one_row)(masses, offsets)
    return lax.reduce_window(segments, jnp.zeros((), segments.dtype), lax.add, (1, TMPL_LEN), (1, 1), 'VALID')

def reference(raw_traces, filter_taps, templates, offsets, channel_mask):
    filtered = filter_traces(raw_traces, filter_taps)
    shaped = shape_templates(templates, channel_mask)

    def one_template(inputs):
        weights, offset_value = inputs
        window = lax.dynamic_slice_in_dim(filtered, offset_value, LAGS + TMPL_LEN - 1, 1)
        product = jnp.dot(weights, window, preferred_element_type=jnp.float32)
        return skew_sum(product, LAGS)
    numerator = lax.map(one_template, (shaped, offsets))
    squares = filtered.astype(jnp.float32) ** 2
    masses = jnp.dot(channel_mask.astype(jnp.float32), squares, precision=lax.Precision.HIGHEST)
    energy = window_energy(masses, offsets, LAGS)
    return numerator / jnp.sqrt(energy)
```

```python
import functools

import jax
import jax.numpy as jnp
from jax import lax
from jax.experimental import pallas as pl
from jax.experimental.pallas import tpu as pltpu
from jax.sharding import PartitionSpec as P

SPAN = 256
BLK = 256
LANE = 128
MESH = pl.DeviceIdType.MESH
PIECES = 1
LEAD = 3
LOANS = 4


def left(x, count):
    size = x.shape[-1]
    count = count % size
    return x if count == 0 else pltpu.roll(x, size - count, x.ndim - 1)


def kernel(
    ntm, nch, npt, lend, share, lead, raw_hbm, taps_hbm, tmpl_hbm, mask_hbm, offs_hbm, out_ref,
    taps_ref, offs_ref, raw, tap_row, tmpl, mask, skewed, shaped, rall, prod, qacc, units, num_out, en_out,
    num_in, en_in, guest, gacc, guest_out, guest_in, own_offs, guest_offs,
    load_sem, raw_sem, recv_sem, right_sem, left_sem,
    unit_right, unit_left, unit_recv, num_send, num_recv, en_send, en_recv,
    loan_send, loan_recv, relay_send, relay_recv, offs_sem, guest_send, guest_recv,
):
    z = lax.axis_index("tmpl")
    c = lax.axis_index("chan")
    p = lax.axis_index("parts")
    rows = raw.shape[0]
    group, tlen, local = tmpl.shape
    nblk = rall.shape[0]
    total = nblk * BLK
    unit = min(LANE, rows)
    nun = rows // unit
    side = ntm // 2 if ntm % 2 == 0 and (ntm // 2 * rows) % LANE == 0 else ntm
    width = side * rows
    near = lax.div(z, side)
    is_end = (z == 0) | (z == ntm - 1)
    is_helper = (z == 1) | (z == ntm - 2)
    inward = jnp.where(z == 0, 1, ntm - 2)
    outward = jnp.where(z == 1, 0, ntm - 1)
    lent = jnp.where(z < ntm - 2, 2, ntm - 3) if ntm != 4 else jnp.where(z < 2, 2, 1)

    def load_raw(n, first):
        at = pl.ds(0, BLK + LANE) if first else pl.ds(pl.multiple_of(n * BLK + LANE, LANE), BLK)
        return pltpu.make_async_copy(raw_hbm.at[:, at], raw.at[:, at], raw_sem.at[n])

    load_taps = pltpu.make_async_copy(taps_hbm, taps_ref, load_sem.at[2])
    load_taps.start()
    for n in range(nblk):
        load_raw(n, n == 0).start()
    loads = [
        pltpu.make_async_copy(tmpl_hbm, tmpl, load_sem.at[0]),
        pltpu.make_async_copy(
            mask_hbm.at[:, pl.ds(pl.multiple_of(c * local, LANE), local)], mask, load_sem.at[1]
        ),
        pltpu.make_async_copy(offs_hbm, offs_ref, load_sem.at[3]),
    ]
    for item in loads:
        item.start()

    barrier = pltpu.get_barrier_semaphore()
    @pl.when(z < ntm - 1)
    def _():
        pl.semaphore_signal(
            barrier, inc=1, device_id={"tmpl": lax.rem(z + 1, ntm)}, device_id_type=MESH
        )

    @pl.when(z > 0)
    def _():
        pl.semaphore_signal(
            barrier, inc=1, device_id={"tmpl": lax.rem(z - 1 + ntm, ntm)}, device_id_type=MESH
        )

    for d in range(1, nch):
        pl.semaphore_signal(
            barrier, inc=1, device_id={"chan": lax.rem(c + d, nch)}, device_id_type=MESH
        )

    if lend:
        @pl.when(is_end)
        def _():
            for d in range(1, nch):
                pl.semaphore_signal(
                    barrier, inc=1,
                    device_id={"chan": lax.rem(c + d, nch), "tmpl": inward}, device_id_type=MESH,
                )

        for e in range(1, share):
            pl.semaphore_signal(
                barrier, inc=1, device_id={"parts": lax.rem(p + e, npt)}, device_id_type=MESH
            )

    tap_row[...] = jnp.zeros_like(tap_row)
    load_taps.wait()
    tap_row[:, : taps_ref.shape[1]] = taps_ref[...]
    band = pltpu.roll(
        jnp.broadcast_to(tap_row[...], (LANE, 2 * LANE)), 0, 1, stride=1, stride_axis=0
    )
    band_hi = band.astype(jnp.bfloat16)
    band_lo = (band - band_hi.astype(jnp.float32)).astype(jnp.bfloat16)
    qacc[...] = jnp.zeros_like(qacc)
    if lend:
        @pl.when(is_end)
        def _():
            at = pl.ds(pl.multiple_of(lent * rows, rows), rows)
            for n in range(nblk):
                rall[n, at, :] = jnp.zeros((rows, BLK), jnp.bfloat16)

        @pl.when(is_helper)
        def _():
            gacc[...] = jnp.zeros_like(gacc)

    load_raw(0, True).wait()

    def chunk(src, n):
        return rall.at[n, pl.ds(pl.multiple_of(src * rows, rows), rows), :]

    def hop(src, n, h, sems, step):
        height = rows // PIECES
        at = pl.ds(pl.multiple_of(src * rows + h * height, height), height)
        return pltpu.make_async_remote_copy(
            src_ref=rall.at[n, at, :],
            dst_ref=rall.at[n, at, :],
            send_sem=sems.at[src, n * PIECES + h],
            recv_sem=recv_sem.at[src, n * PIECES + h],
            device_id={"tmpl": lax.rem(z + step + ntm, ntm)},
            device_id_type=MESH,
        )

    def contract(a, b):
        return lax.dot_general(
            a, b, (((1,), (1,)), ((), ())), preferred_element_type=jnp.float32
        )

    def fir(n, carry):
        x = raw[:, pl.ds(pl.multiple_of(n * BLK, BLK), BLK + LANE)]
        hi = x.astype(jnp.bfloat16)
        lo = (x - hi.astype(jnp.float32)).astype(jnp.bfloat16)
        for half in range(BLK // LANE):
            a = hi[:, half * LANE : half * LANE + 2 * LANE]
            b = lo[:, half * LANE : half * LANE + 2 * LANE]
            y = contract(a, band_hi) + (contract(b, band_hi) + contract(a, band_lo))
            y = y.astype(jnp.bfloat16)
            rall[
                n, pl.ds(pl.multiple_of(z * rows, rows), rows), half * LANE : half * LANE + LANE
            ] = y
            y = y.astype(jnp.float32)
            y = y * y
            at = pl.ds(pl.multiple_of(n * BLK + half * LANE, LANE), LANE)
            for u in range(nun):
                units[z, u : u + 1, at] = jnp.sum(
                    y[u * unit : (u + 1) * unit], axis=0, keepdims=True
                )

        return carry

    def send_right(src, n):
        for h in range(PIECES):
            hop(src, n, h, right_sem, 1).start()

    def send_left(src, n):
        for h in range(PIECES):
            hop(src, n, h, left_sem, -1).start()

    goes_right = z < ntm - 1
    goes_left = z > 0
    held_right = (z == 1) & (lead < nblk)
    held_left = (z == ntm - 2) & (lead < nblk)

    def send_own(n, carry):
        @pl.when(goes_right & ((n < lead) | jnp.logical_not(held_right)))
        def _():
            send_right(z, n)

        @pl.when(goes_left & ((n < lead) | jnp.logical_not(held_left)))
        def _():
            send_left(z, n)

        return carry

    def send_held(n, carry):
        @pl.when(held_right)
        def _():
            send_right(z, n)

        @pl.when(held_left)
        def _():
            send_left(z, n)

        return carry

    def fir_next(n, carry):
        load_raw(n, False).wait()
        return fir(n, carry)

    def unit_hop(src, sems, step):
        return pltpu.make_async_remote_copy(
            src_ref=units.at[src],
            dst_ref=units.at[src],
            send_sem=sems.at[src],
            recv_sem=unit_recv.at[src],
            device_id={"tmpl": lax.rem(z + step + ntm, ntm)},
            device_id_type=MESH,
        )

    fir(0, 0)
    pl.semaphore_wait(
        barrier,
        jnp.where(z < ntm - 1, 1, 0) + jnp.where(z > 0, 1, 0) + (nch - 1)
        + (jnp.where(is_helper, nch - 1, 0) + (share - 1) if lend else 0),
    )
    send_own(0, 0)
    lax.fori_loop(1, nblk, fir_next, 0)

    @pl.when(z < ntm - 1)
    def _():
        unit_hop(z, unit_right, 1).start()

    @pl.when(z > 0)
    def _():
        unit_hop(z, unit_left, -1).start()

    lax.fori_loop(1, nblk, send_own, 0)

    for item in loads:
        item.wait()

    def shape_cols(i, carry):
        cols = pl.ds(pl.multiple_of(i * LANE, LANE), LANE)
        flags = mask[:, cols].astype(jnp.float32)
        for k in range(group):
            v = tmpl[k, :, cols].astype(jnp.float32)
            power = jnp.mean(v * v, axis=0, keepdims=True)
            scale = flags[k : k + 1, :] / jnp.sqrt(power + 1e-06)
            skewed[pl.ds(k, tlen, stride=group), :] = v * scale
        shaped[:, cols] = skewed[...].astype(jnp.bfloat16)
        return carry

    lines = tlen * group // share
    cuts = [lines // 16 * j // LOANS * 16 for j in range(LOANS)] + [lines]

    def loan_lines(owner, j):
        return pl.ds(pl.multiple_of(owner * lines + cuts[j], 16), cuts[j + 1] - cuts[j])

    def loan(j, peer):
        owner = lax.rem(p, share)
        at = loan_lines(owner, j)
        return pltpu.make_async_remote_copy(
            src_ref=shaped.at[at, pl.ds(pl.multiple_of(lent * rows, rows), rows)],
            dst_ref=guest.at[at, :],
            send_sem=loan_send.at[j],
            recv_sem=loan_recv.at[j],
            device_id={"tmpl": peer},
            device_id_type=MESH,
        )

    def relay(e, j, owner):
        at = loan_lines(owner, j)
        return pltpu.make_async_remote_copy(
            src_ref=guest.at[at, :],
            dst_ref=guest.at[at, :],
            send_sem=relay_send.at[e, j],
            recv_sem=relay_recv.at[e, j],
            device_id={"parts": lax.rem(p + e, npt)},
            device_id_type=MESH,
        )

    def offs_copy(peer):
        return pltpu.make_async_remote_copy(
            src_ref=own_offs,
            dst_ref=guest_offs,
            send_sem=offs_sem.at[0],
            recv_sem=offs_sem.at[1],
            device_id={"tmpl": peer},
            device_id_type=MESH,
        )

    offs = jnp.zeros((group, 1), jnp.int32)
    index = lax.broadcasted_iota(jnp.int32, (group, 1), 0)
    for k in range(group):
        offs = jnp.where(index == k, offs_ref[k], offs)

    per = width // LANE
    if lend:
        @pl.when(is_end)
        def _():
            own_offs[...] = jnp.broadcast_to(offs, own_offs.shape)
            first = lent * (rows // LANE)
            lax.fori_loop(first, first + rows // LANE, shape_cols, 0)
            for j in range(LOANS):
                loan(j, inward).start()
            offs_copy(inward).start()

    lax.fori_loop(near * per, near * per + per, shape_cols, 0)

    def shape_rest():
        first = (1 - near) * per

        def body(i, carry):
            if lend:
                skip = is_end & (lax.div(i, rows // LANE) == lent)

                @pl.when(jnp.logical_not(skip))
                def _():
                    shape_cols(i, 0)
            else:
                shape_cols(i, 0)
            return carry

        lax.fori_loop(first, first + per, body, 0)

    def shift_rows(x, by):
        amount = jnp.broadcast_to(by, x.shape)
        bit = 1
        while bit < SPAN - tlen + 1:
            x = jnp.where((amount & bit) != 0, left(x, bit), x)
            bit *= 2
        return x

    def spread(x, own_ref, in_ref, send, recv):
        lag = own_ref.shape[2]
        for j in range(nch):
            own_ref[j] = x[:, j * lag : (j + 1) * lag]
        for d in range(1, nch):
            other = lax.rem(c + d, nch)
            pltpu.make_async_remote_copy(
                src_ref=own_ref.at[other],
                dst_ref=in_ref.at[d],
                send_sem=send.at[d],
                recv_sem=recv.at[d],
                device_id={"chan": other},
                device_id_type=MESH,
            ).start()

    def collect(own_ref, in_ref, send, recv):
        value = own_ref[c]
        for d in range(1, nch):
            pltpu.make_async_remote_copy(
                src_ref=own_ref.at[lax.rem(c + d, nch)],
                dst_ref=in_ref.at[d],
                send_sem=send.at[d],
                recv_sem=recv.at[d],
                device_id={"chan": lax.rem(c + d, nch)},
                device_id_type=MESH,
            ).wait()
            value = value + in_ref[d]
        return value

    def unit_arrive(d):
        @pl.when(z - d >= 0)
        def _():
            src = lax.rem(z - d + ntm, ntm)
            unit_hop(src, unit_right, 1).wait_recv()

            @pl.when(z < ntm - 1)
            def _():
                unit_hop(src, unit_right, 1).start()

        @pl.when(z + d < ntm)
        def _():
            src = lax.rem(z + d, ntm)
            unit_hop(src, unit_left, -1).wait_recv()

            @pl.when(z > 0)
            def _():
                unit_hop(src, unit_left, -1).start()

    def send_energy():
        masses = jnp.zeros((group, total), jnp.float32)
        for s in range(ntm):
            for u in range(nun):
                at = s * rows + u * unit
                flag = mask[:, at : at + 1].astype(jnp.float32)
                masses = masses + flag * units[s, u : u + 1, :]
        window, width, place, energy = masses, 1, 0, None
        while width <= tlen:
            if tlen & width:
                piece = left(window, place)
                energy = piece if energy is None else energy + piece
                place += width
            window = window + left(window, width)
            width *= 2
        spread(shift_rows(energy, offs), en_out, en_in, en_send, en_recv)

    def arrive(d, n, same):
        def fits(src):
            return (lax.div(src, side) == near) == same

        @pl.when(
            (z - d >= 0) & fits(lax.rem(z - d + ntm, ntm))
            & ((z < ntm - 1) if lend and d == 2 else True)
        )
        def _():
            src = lax.rem(z - d + ntm, ntm)
            for h in range(PIECES):
                hop(src, n, h, right_sem, 1).wait_recv()

                @pl.when(z < ntm - 1 - (1 if lend and d == 1 else 0))
                def _():
                    hop(src, n, h, right_sem, 1).start()

        @pl.when(
            (z + d < ntm) & fits(lax.rem(z + d, ntm)) & ((z > 0) if lend and d == 2 else True)
        )
        def _():
            src = lax.rem(z + d, ntm)
            for h in range(PIECES):
                hop(src, n, h, left_sem, -1).wait_recv()

                @pl.when(z > (1 if lend and d == 1 else 0))
                def _():
                    hop(src, n, h, left_sem, -1).start()

    def arrive_far(n):
        for d in range(2, ntm):
            arrive(d, n, False)

    def skew(n, weights, samples, acc, begin, end):
        prod[: weights.shape[0], :] = jnp.dot(
            weights, samples, preferred_element_type=jnp.float32
        )
        blank = jnp.zeros((group, LANE), jnp.float32)
        total_acc = jnp.zeros((group, 2 * BLK), jnp.float32)

        def row(tap):
            if tap < begin or tap >= end:
                return None
            line = (tap - begin) * group
            return prod[line : line + group, :]

        for g in range(min(LANE, tlen)):
            low, high = row(g), row(g + LANE)
            if low is None and high is None:
                continue
            carry_in, first, second = blank, blank, blank
            if low is not None:
                first, second = low[:, :LANE], low[:, LANE:]
            if high is not None:
                carry_in = high[:, :LANE]
                first = high[:, LANE:] if low is None else first + high[:, LANE:]
            wide = jnp.concatenate([blank, carry_in, first, second], axis=1)
            total_acc = total_acc + left(wide, g)
        at = pl.ds(pl.multiple_of(n * BLK, BLK), 2 * BLK)
        acc[:, at] = acc[:, at] + total_acc

    def half_block(which, n):
        at = pl.ds(pl.multiple_of(which * width, width), width)
        skew(n, shaped[:, at], rall[n, at, :], qacc, 0, tlen)

    def guest_block(n, carry):
        skew(n, guest[...], chunk(lent, n)[...], gacc, 0, tlen)
        return carry

    def guest_copy(d, peer):
        other = lax.rem(c + d, nch)
        return pltpu.make_async_remote_copy(
            src_ref=guest_out.at[other],
            dst_ref=guest_in.at[d],
            send_sem=guest_send.at[d],
            recv_sem=guest_recv.at[d],
            device_id={"chan": other, "tmpl": peer},
            device_id_type=MESH,
        )

    def near_round(n, carry):
        for d in range(1, side):
            arrive(d, n, True)

        @pl.when(n == 0)
        def _():
            unit_arrive(1)

        if side < ntm and lead < nblk:
            @pl.when(n >= lead)
            def _():
                arrive_far(n - lead)

        @pl.when(n == nblk - 1)
        def _():
            lax.fori_loop(lead, nblk, send_held, 0)
            if ntm > 2:
                unit_arrive(2)

        half_block(near, n)
        if side < ntm:
            @pl.when(n == 0)
            def _():
                shape_rest()

        return carry

    def far_round(n, carry):
        @pl.when(n < lead)
        def _():
            arrive(1, n, False)

        @pl.when(n >= (nblk - lead if lead < nblk else 0))
        def _():
            arrive_far(n)

        @pl.when(n == min(2, nblk - 1))
        def _():
            for d in range(3, ntm):
                unit_arrive(d)
            send_energy()

        if lend:
            for j in range(LOANS):
                @pl.when(is_helper & (n == max(0, nblk - LOANS + j)))
                def _():
                    loan(j, outward).wait_recv()
                    for e in range(1, share):
                        relay(e, j, p).start()

        @pl.when((n < lead) | jnp.logical_not(is_helper))
        def _():
            half_block(1 - near, n)

        return carry

    def last_round(n, carry):
        arrive(1, n, False)

        @pl.when(is_helper)
        def _():
            guest_block(n, 0)

            @pl.when(n == nblk - 1)
            def _():
                moved = shift_rows(gacc[:, BLK:], guest_offs[:, :1])
                lag = guest_out.shape[2]
                for j in range(nch):
                    guest_out[j] = moved[:, j * lag : (j + 1) * lag]
                for d in range(nch):
                    guest_copy(d, outward).start()

            half_block(1 - near, n)

        return carry

    lax.fori_loop(0, nblk, near_round, 0)
    if side < ntm:
        lax.fori_loop(0, nblk, far_round, 0)
    else:
        for d in range(3, ntm):
            unit_arrive(d)
        send_energy()

    if lend:
        @pl.when(is_helper)
        def _():
            offs_copy(outward).wait_recv()
            for j in range(LOANS):
                for e in range(1, share):
                    relay(e, j, lax.rem(p - e + npt, npt)).wait_recv()
            lax.fori_loop(0, lead, guest_block, 0)

        lax.fori_loop(lead, nblk, last_round, 0)

    spread(shift_rows(qacc[:, BLK:], offs), num_out, num_in, num_send, num_recv)

    def drain(n, carry):
        for s in range(ntm):
            @pl.when(
                (s <= z) & (z < ntm - 1)
                & (((z != ntm - 2) | (s != ntm - 3)) if lend else True)
            )
            def _():
                for h in range(PIECES):
                    hop(s, n, h, right_sem, 1).wait_send()

            @pl.when((s >= z) & (z > 0) & (((z != 1) | (s != 2)) if lend else True))
            def _():
                for h in range(PIECES):
                    hop(s, n, h, left_sem, -1).wait_send()

        return carry

    lax.fori_loop(0, nblk, drain, 0)
    for s in range(ntm):
        @pl.when((s <= z) & (z < ntm - 1))
        def _():
            unit_hop(s, unit_right, 1).wait_send()

        @pl.when((s >= z) & (z > 0))
        def _():
            unit_hop(s, unit_left, -1).wait_send()

    if lend:
        @pl.when(is_end)
        def _():
            for j in range(LOANS):
                loan(j, inward).wait_send()
            offs_copy(inward).wait_send()

        @pl.when(is_helper)
        def _():
            for j in range(LOANS):
                for e in range(1, share):
                    relay(e, j, p).wait_send()

    energy = collect(en_out, en_in, en_send, en_recv)
    numerator = collect(num_out, num_in, num_send, num_recv)
    if lend:
        num_out[0] = numerator

        @pl.when(is_end)
        def _():
            total_in = num_out[0]
            for d in range(nch):
                guest_copy(d, inward).wait_recv()
                total_in = total_in + guest_in[d]
            num_out[0] = total_in

        @pl.when(is_helper)
        def _():
            for d in range(nch):
                guest_copy(d, outward).wait_send()

        numerator = num_out[0]
    out_ref[...] = numerator / jnp.sqrt(energy)


def shards(raw_traces, filter_taps, templates, offsets, channel_mask):
    ntm = lax.axis_size("tmpl")
    nch = lax.axis_size("chan")
    rows, length = raw_traces.shape
    group, tlen, local = templates.shape
    nblk = (length - filter_taps.shape[0] + 1) // BLK
    total = nblk * BLK
    lag = (total - SPAN) // nch
    nun = rows // min(LANE, rows)
    npt = lax.axis_size("parts")
    lend = int(ntm == 4 and rows % LANE == 0 and nblk >= LOANS)
    share = npt if lend and group * tlen % (16 * npt) == 0 else 1
    lead = min(LEAD, nblk - 1) if lend else nblk
    f32, bf16, dma = jnp.float32, jnp.bfloat16, pltpu.SemaphoreType.DMA
    any_spec = pl.BlockSpec(memory_space=pl.ANY)
    vmem_spec = pl.BlockSpec(memory_space=pltpu.VMEM)
    return pl.pallas_call(
        functools.partial(kernel, ntm, nch, npt, lend, share, lead),
        out_shape=jax.ShapeDtypeStruct((group, lag), f32),
        in_specs=[
            any_spec, any_spec, any_spec, any_spec, any_spec,
        ],
        out_specs=vmem_spec,
        scratch_shapes=[
            pltpu.VMEM((1, filter_taps.shape[0]), f32),
            pltpu.SMEM((group,), jnp.int32),
            pltpu.VMEM((rows, length), f32),
            pltpu.VMEM((1, 2 * LANE), f32),
            pltpu.VMEM((group, tlen, local), bf16),
            pltpu.VMEM((group, local), jnp.int32),
            pltpu.VMEM((group * tlen, LANE), f32),
            pltpu.VMEM((group * tlen, local), bf16),
            pltpu.VMEM((nblk, local, BLK), bf16),
            pltpu.VMEM((group * tlen, BLK), f32),
            pltpu.VMEM((group, BLK + total), f32),
            pltpu.VMEM((ntm, nun, total), f32),
            pltpu.VMEM((nch, group, lag), f32),
            pltpu.VMEM((nch, group, lag), f32),
            pltpu.VMEM((nch, group, lag), f32),
            pltpu.VMEM((nch, group, lag), f32),
            pltpu.VMEM((group * tlen, rows if lend else LANE), bf16),
            pltpu.VMEM((group, BLK + total), f32),
            pltpu.VMEM((nch, group, lag), f32),
            pltpu.VMEM((nch, group, lag), f32),
            pltpu.VMEM((group, LANE), jnp.int32),
            pltpu.VMEM((group, LANE), jnp.int32),
            dma((4,)),
            dma((nblk,)),
            dma((ntm, nblk * PIECES)),
            dma((ntm, nblk * PIECES)),
            dma((ntm, nblk * PIECES)),
            dma((ntm,)),
            dma((ntm,)),
            dma((ntm,)),
            dma((nch,)),
            dma((nch,)),
            dma((nch,)),
            dma((nch,)),
            dma((LOANS,)),
            dma((LOANS,)),
            dma((npt, LOANS)),
            dma((npt, LOANS)),
            dma((2,)),
            dma((nch,)),
            dma((nch,)),
        ],
        compiler_params=pltpu.CompilerParams(
            collective_id=0, has_side_effects=True, vmem_limit_bytes=60 * 1024 * 1024
        ),
    )(raw_traces, filter_taps.reshape(1, -1), templates, channel_mask, offsets)


def solution(mesh):
    placed = (
        P(("chan", "tmpl"), "parts"),
        P(),
        P("tmpl", None, "chan"),
        P("tmpl"),
        P("tmpl", None),
    )
    return jax.shard_map(
        shards, mesh=mesh, in_specs=placed, out_specs=P("tmpl", ("parts", "chan")), check_vma=False
    )
```

```python
import functools

import jax
import jax.numpy as jnp
from jax import lax
from jax.experimental import pallas as pl
from jax.experimental.pallas import tpu as pltpu
from jax.sharding import PartitionSpec as P

SPAN = 256
BLK = 256
LANE = 128
MESH = pl.DeviceIdType.MESH
PIECES = 1
LEAD = 3
LOANS = (16, 16, 15, 14, 13, 11, 9, 6)


def left(x, count):
    size = x.shape[-1]
    count = count % size
    return x if count == 0 else pltpu.roll(x, size - count, x.ndim - 1)


def kernel(
    ntm, nch, npt, lend, share, lead, raw_hbm, taps_hbm, tmpl_hbm, mask_hbm, offs_hbm, out_ref,
    taps_ref, offs_ref, raw, tap_row, tmpl, mask, skewed, shaped, rall, prod, qacc, units, num_out, en_out,
    num_in, en_in, guest, gacc, guest_out, guest_in, own_offs, guest_offs,
    load_sem, raw_sem, recv_sem, right_sem, left_sem,
    unit_right, unit_left, unit_recv, num_send, num_recv, en_send, en_recv,
    loan_send, loan_recv, relay_send, relay_recv, offs_sem, guest_send, guest_recv,
):
    z = lax.axis_index("tmpl")
    c = lax.axis_index("chan")
    p = lax.axis_index("parts")
    rows = raw.shape[0]
    group, tlen, local = tmpl.shape
    nblk = rall.shape[0]
    total = nblk * BLK
    unit = min(LANE, rows)
    nun = rows // unit
    side = ntm // 2 if ntm % 2 == 0 and (ntm // 2 * rows) % LANE == 0 else ntm
    width = side * rows
    near = lax.div(z, side)
    is_end = (z == 0) | (z == ntm - 1)
    is_helper = (z == 1) | (z == ntm - 2)
    inward = jnp.where(z == 0, 1, ntm - 2)
    outward = jnp.where(z == 1, 0, ntm - 1)
    lent = jnp.where(z < ntm - 2, 2, ntm - 3) if ntm != 4 else jnp.where(z < 2, 2, 1)

    def load_raw(n, first):
        at = pl.ds(0, BLK + LANE) if first else pl.ds(pl.multiple_of(n * BLK + LANE, LANE), BLK)
        return pltpu.make_async_copy(raw_hbm.at[:, at], raw.at[:, at], raw_sem.at[n])

    load_taps = pltpu.make_async_copy(taps_hbm, taps_ref, load_sem.at[2])
    load_taps.start()
    for n in range(nblk):
        load_raw(n, n == 0).start()
    loads = [
        pltpu.make_async_copy(tmpl_hbm, tmpl, load_sem.at[0]),
        pltpu.make_async_copy(
            mask_hbm.at[:, pl.ds(pl.multiple_of(c * local, LANE), local)], mask, load_sem.at[1]
        ),
        pltpu.make_async_copy(offs_hbm, offs_ref, load_sem.at[3]),
    ]
    for item in loads:
        item.start()

    barrier = pltpu.get_barrier_semaphore()
    @pl.when(z < ntm - 1)
    def _():
        pl.semaphore_signal(
            barrier, inc=1, device_id={"tmpl": lax.rem(z + 1, ntm)}, device_id_type=MESH
        )

    @pl.when(z > 0)
    def _():
        pl.semaphore_signal(
            barrier, inc=1, device_id={"tmpl": lax.rem(z - 1 + ntm, ntm)}, device_id_type=MESH
        )

    for d in range(1, nch):
        pl.semaphore_signal(
            barrier, inc=1, device_id={"chan": lax.rem(c + d, nch)}, device_id_type=MESH
        )

    if lend:
        @pl.when(is_end)
        def _():
            for d in range(1, nch):
                pl.semaphore_signal(
                    barrier, inc=1,
                    device_id={"chan": lax.rem(c + d, nch), "tmpl": inward}, device_id_type=MESH,
                )

        for e in range(1, share):
            pl.semaphore_signal(
                barrier, inc=1, device_id={"parts": lax.rem(p + e, npt)}, device_id_type=MESH
            )

    tap_row[...] = jnp.zeros_like(tap_row)
    load_taps.wait()
    tap_row[:, : taps_ref.shape[1]] = taps_ref[...]
    band = pltpu.roll(
        jnp.broadcast_to(tap_row[...], (LANE, 2 * LANE)), 0, 1, stride=1, stride_axis=0
    )
    band_hi = band.astype(jnp.bfloat16)
    band_lo = (band - band_hi.astype(jnp.float32)).astype(jnp.bfloat16)
    qacc[...] = jnp.zeros_like(qacc)
    if lend:
        @pl.when(is_end)
        def _():
            at = pl.ds(pl.multiple_of(lent * rows, rows), rows)
            for n in range(nblk):
                rall[n, at, :] = jnp.zeros((rows, BLK), jnp.bfloat16)

        @pl.when(is_helper)
        def _():
            gacc[...] = jnp.zeros_like(gacc)

    load_raw(0, True).wait()

    def chunk(src, n):
        return rall.at[n, pl.ds(pl.multiple_of(src * rows, rows), rows), :]

    def hop(src, n, h, sems, step):
        height = rows // PIECES
        at = pl.ds(pl.multiple_of(src * rows + h * height, height), height)
        return pltpu.make_async_remote_copy(
            src_ref=rall.at[n, at, :],
            dst_ref=rall.at[n, at, :],
            send_sem=sems.at[src, n * PIECES + h],
            recv_sem=recv_sem.at[src, n * PIECES + h],
            device_id={"tmpl": lax.rem(z + step + ntm, ntm)},
            device_id_type=MESH,
        )

    def contract(a, b):
        return lax.dot_general(
            a, b, (((1,), (1,)), ((), ())), preferred_element_type=jnp.float32
        )

    def fir(n, carry):
        x = raw[:, pl.ds(pl.multiple_of(n * BLK, BLK), BLK + LANE)]
        hi = x.astype(jnp.bfloat16)
        lo = (x - hi.astype(jnp.float32)).astype(jnp.bfloat16)
        for half in range(BLK // LANE):
            a = hi[:, half * LANE : half * LANE + 2 * LANE]
            b = lo[:, half * LANE : half * LANE + 2 * LANE]
            y = contract(a, band_hi) + (contract(b, band_hi) + contract(a, band_lo))
            y = y.astype(jnp.bfloat16)
            rall[
                n, pl.ds(pl.multiple_of(z * rows, rows), rows), half * LANE : half * LANE + LANE
            ] = y
            y = y.astype(jnp.float32)
            y = y * y
            at = pl.ds(pl.multiple_of(n * BLK + half * LANE, LANE), LANE)
            for u in range(nun):
                units[z, u : u + 1, at] = jnp.sum(
                    y[u * unit : (u + 1) * unit], axis=0, keepdims=True
                )

        return carry

    def send_right(src, n):
        for h in range(PIECES):
            hop(src, n, h, right_sem, 1).start()

    def send_left(src, n):
        for h in range(PIECES):
            hop(src, n, h, left_sem, -1).start()

    goes_right = z < ntm - 1
    goes_left = z > 0
    held_right = (z == 1) & (lead < nblk)
    held_left = (z == ntm - 2) & (lead < nblk)

    def send_own(n, carry):
        @pl.when(goes_right & ((n < lead) | jnp.logical_not(held_right)))
        def _():
            send_right(z, n)

        @pl.when(goes_left & ((n < lead) | jnp.logical_not(held_left)))
        def _():
            send_left(z, n)

        return carry

    def send_held(n, carry):
        @pl.when(held_right)
        def _():
            send_right(z, n)

        @pl.when(held_left)
        def _():
            send_left(z, n)

        return carry

    def fir_next(n, carry):
        load_raw(n, False).wait()
        return fir(n, carry)

    def unit_hop(src, sems, step):
        return pltpu.make_async_remote_copy(
            src_ref=units.at[src],
            dst_ref=units.at[src],
            send_sem=sems.at[src],
            recv_sem=unit_recv.at[src],
            device_id={"tmpl": lax.rem(z + step + ntm, ntm)},
            device_id_type=MESH,
        )

    fir(0, 0)
    pl.semaphore_wait(
        barrier,
        jnp.where(z < ntm - 1, 1, 0) + jnp.where(z > 0, 1, 0) + (nch - 1)
        + (jnp.where(is_helper, nch - 1, 0) + (share - 1) if lend else 0),
    )
    send_own(0, 0)
    lax.fori_loop(1, nblk, fir_next, 0)

    @pl.when(z < ntm - 1)
    def _():
        unit_hop(z, unit_right, 1).start()

    @pl.when(z > 0)
    def _():
        unit_hop(z, unit_left, -1).start()

    lax.fori_loop(1, nblk, send_own, 0)
    for item in loads:
        item.wait()

    def shape_cols(i, carry):
        cols = pl.ds(pl.multiple_of(i * LANE, LANE), LANE)
        flags = mask[:, cols].astype(jnp.float32)
        for k in range(group):
            v = tmpl[k, :, cols].astype(jnp.float32)
            power = jnp.mean(v * v, axis=0, keepdims=True)
            scale = flags[k : k + 1, :] / jnp.sqrt(power + 1e-06)
            skewed[pl.ds(k, tlen, stride=group), :] = v * scale
        shaped[:, cols] = skewed[...].astype(jnp.bfloat16)
        return carry

    lines = tlen * group // share
    npc = len(LOANS)
    cuts = [lines // 16 * sum(LOANS[:j]) // sum(LOANS) * 16 for j in range(npc)] + [lines]

    def loan_lines(owner, j):
        return pl.ds(pl.multiple_of(owner * lines + cuts[j], 16), cuts[j + 1] - cuts[j])

    def loan(j, peer):
        owner = lax.rem(p, share)
        at = loan_lines(owner, j)
        return pltpu.make_async_remote_copy(
            src_ref=shaped.at[at, pl.ds(pl.multiple_of(lent * rows, rows), rows)],
            dst_ref=guest.at[at, :],
            send_sem=loan_send.at[j],
            recv_sem=loan_recv.at[j],
            device_id={"tmpl": peer},
            device_id_type=MESH,
        )

    def relay(e, j, owner):
        at = loan_lines(owner, j)
        return pltpu.make_async_remote_copy(
            src_ref=guest.at[at, :],
            dst_ref=guest.at[at, :],
            send_sem=relay_send.at[e, j],
            recv_sem=relay_recv.at[e, j],
            device_id={"parts": lax.rem(p + e, npt)},
            device_id_type=MESH,
        )

    def offs_copy(peer):
        return pltpu.make_async_remote_copy(
            src_ref=own_offs,
            dst_ref=guest_offs,
            send_sem=offs_sem.at[0],
            recv_sem=offs_sem.at[1],
            device_id={"tmpl": peer},
            device_id_type=MESH,
        )

    offs = jnp.zeros((group, 1), jnp.int32)
    index = lax.broadcasted_iota(jnp.int32, (group, 1), 0)
    for k in range(group):
        offs = jnp.where(index == k, offs_ref[k], offs)

    per = width // LANE
    ahead = rows // LANE if lend else 0
    if lend:
        first = jnp.where(is_end, lent * ahead, near * per)
        lax.fori_loop(first, first + ahead, shape_cols, 0)
        own_offs[...] = jnp.broadcast_to(offs, own_offs.shape)

    if lend:
        @pl.when(is_end)
        def _():
            for j in range(npc):
                loan(j, inward).start()
            offs_copy(inward).start()

    lax.fori_loop(near * per + jnp.where(is_end, 0, ahead), near * per + per, shape_cols, 0)

    def shape_rest():
        first = (1 - near) * per

        def body(i, carry):
            if lend:
                skip = is_end & (lax.div(i, rows // LANE) == lent)

                @pl.when(jnp.logical_not(skip))
                def _():
                    shape_cols(i, 0)
            else:
                shape_cols(i, 0)
            return carry

        lax.fori_loop(first, first + per, body, 0)

    def shift_rows(x, by):
        amount = jnp.broadcast_to(by, x.shape)
        bit = 1
        while bit < SPAN - tlen + 1:
            x = jnp.where((amount & bit) != 0, left(x, bit), x)
            bit *= 2
        return x

    def spread(x, own_ref, in_ref, send, recv):
        lag = own_ref.shape[2]
        for j in range(nch):
            own_ref[j] = x[:, j * lag : (j + 1) * lag]
        for d in range(1, nch):
            other = lax.rem(c + d, nch)
            pltpu.make_async_remote_copy(
                src_ref=own_ref.at[other],
                dst_ref=in_ref.at[d],
                send_sem=send.at[d],
                recv_sem=recv.at[d],
                device_id={"chan": other},
                device_id_type=MESH,
            ).start()

    def collect(own_ref, in_ref, send, recv):
        value = own_ref[c]
        for d in range(1, nch):
            pltpu.make_async_remote_copy(
                src_ref=own_ref.at[lax.rem(c + d, nch)],
                dst_ref=in_ref.at[d],
                send_sem=send.at[d],
                recv_sem=recv.at[d],
                device_id={"chan": lax.rem(c + d, nch)},
                device_id_type=MESH,
            ).wait()
            value = value + in_ref[d]
        return value

    def unit_arrive(d):
        @pl.when(z - d >= 0)
        def _():
            src = lax.rem(z - d + ntm, ntm)
            unit_hop(src, unit_right, 1).wait_recv()

            @pl.when(z < ntm - 1)
            def _():
                unit_hop(src, unit_right, 1).start()

        @pl.when(z + d < ntm)
        def _():
            src = lax.rem(z + d, ntm)
            unit_hop(src, unit_left, -1).wait_recv()

            @pl.when(z > 0)
            def _():
                unit_hop(src, unit_left, -1).start()

    def send_energy():
        masses = jnp.zeros((group, total), jnp.float32)
        for s in range(ntm):
            for u in range(nun):
                at = s * rows + u * unit
                flag = mask[:, at : at + 1].astype(jnp.float32)
                masses = masses + flag * units[s, u : u + 1, :]
        window, width, place, energy = masses, 1, 0, None
        while width <= tlen:
            if tlen & width:
                piece = left(window, place)
                energy = piece if energy is None else energy + piece
                place += width
            window = window + left(window, width)
            width *= 2
        spread(shift_rows(energy, offs), en_out, en_in, en_send, en_recv)

    def arrive(d, n, same):
        def fits(src):
            return (lax.div(src, side) == near) == same

        @pl.when(
            (z - d >= 0) & fits(lax.rem(z - d + ntm, ntm))
            & ((z < ntm - 1) if lend and d == 2 else True)
        )
        def _():
            src = lax.rem(z - d + ntm, ntm)
            for h in range(PIECES):
                hop(src, n, h, right_sem, 1).wait_recv()

                @pl.when(z < ntm - 1 - (1 if lend and d == 1 else 0))
                def _():
                    hop(src, n, h, right_sem, 1).start()

        @pl.when(
            (z + d < ntm) & fits(lax.rem(z + d, ntm)) & ((z > 0) if lend and d == 2 else True)
        )
        def _():
            src = lax.rem(z + d, ntm)
            for h in range(PIECES):
                hop(src, n, h, left_sem, -1).wait_recv()

                @pl.when(z > (1 if lend and d == 1 else 0))
                def _():
                    hop(src, n, h, left_sem, -1).start()

    def arrive_far(n):
        for d in range(2, ntm):
            arrive(d, n, False)

    def skew(n, weights, samples, acc, begin, end):
        prod[: weights.shape[0], :] = jnp.dot(
            weights, samples, preferred_element_type=jnp.float32
        )
        blank = jnp.zeros((group, LANE), jnp.float32)
        span = end - begin
        reach = BLK + (2 * LANE if span > LANE else LANE)
        total_acc = jnp.zeros((group, reach), jnp.float32)

        def row(tap):
            if tap < begin or tap >= end:
                return None
            line = (tap - begin) * group
            return prod[line : line + group, :]

        for g in range(min(LANE, span)):
            low, high = row(g), row(g + LANE)
            if low is None and high is None:
                continue
            carry_in, first, second = blank, blank, blank
            if low is not None:
                first, second = low[:, :LANE], low[:, LANE:]
            if high is not None:
                carry_in = high[:, :LANE]
                first = high[:, LANE:] if low is None else first + high[:, LANE:]
            if span > LANE:
                wide = jnp.concatenate([blank, carry_in, first, second], axis=1)
            else:
                wide = jnp.concatenate([blank, first, second], axis=1)
            total_acc = total_acc + left(wide, g)
        at = pl.ds(pl.multiple_of(n * BLK + 2 * BLK - reach, LANE), reach)
        acc[:, at] = acc[:, at] + total_acc

    def half_block(which, n):
        at = pl.ds(pl.multiple_of(which * width, width), width)
        skew(n, shaped[:, at], rall[n, at, :], qacc, 0, tlen)

    def guest_block(n, carry):
        skew(n, guest[...], chunk(lent, n)[...], gacc.at[0], 0, tlen)
        return carry

    def guest_share(owner, n):
        at = pl.ds(pl.multiple_of(owner * lines, 16), lines)
        skew(n, guest[at, :], chunk(lent, n)[...], gacc.at[owner], 0, tlen // share)

    def guest_copy(d, peer):
        other = lax.rem(c + d, nch)
        return pltpu.make_async_remote_copy(
            src_ref=guest_out.at[other],
            dst_ref=guest_in.at[d],
            send_sem=guest_send.at[d],
            recv_sem=guest_recv.at[d],
            device_id={"chan": other, "tmpl": peer},
            device_id_type=MESH,
        )

    def near_round(n, carry):
        for d in range(1, side):
            arrive(d, n, True)

        @pl.when(n == 0)
        def _():
            unit_arrive(1)

        if side < ntm and lead < nblk:
            @pl.when(n >= lead)
            def _():
                arrive_far(n - lead)

        @pl.when(n == nblk - 1)
        def _():
            lax.fori_loop(lead, nblk, send_held, 0)
            if ntm > 2:
                unit_arrive(2)

        half_block(near, n)
        if side < ntm:
            @pl.when(n == 0)
            def _():
                shape_rest()

        return carry

    def far_round(n, carry):
        @pl.when(n < lead)
        def _():
            arrive(1, n, False)

        @pl.when(n >= (nblk - lead if lead < nblk else 0))
        def _():
            arrive_far(n)

        @pl.when(n == min(2, nblk - 1))
        def _():
            for d in range(3, ntm):
                unit_arrive(d)
            send_energy()

        @pl.when((n < lead) | jnp.logical_not(is_helper))
        def _():
            half_block(1 - near, n)

        if lend:
            for j in range(npc):
                @pl.when(is_helper & (n == min(nblk - 1, 1 + (2 * j + 1) * 8 // (5 * npc))))
                def _():
                    loan(j, outward).wait_recv()
                    for e in range(1, share):
                        relay(e, j, p).start()

        return carry

    def held_round(n, carry):
        arrive(1, n, False)
        half_block(1 - near, n)
        return carry

    def finish_guest():
        moved = gacc[0, :, BLK:]
        if share > 1:
            for q in range(1, share):
                moved = moved + left(gacc[q], q * tlen // share)[:, BLK:]
        moved = shift_rows(moved, guest_offs[:, :1])
        lag = guest_out.shape[2]
        for j in range(nch):
            guest_out[j] = moved[:, j * lag : (j + 1) * lag]
        for d in range(nch):
            guest_copy(d, outward).start()

    lax.fori_loop(0, nblk, near_round, 0)
    if side < ntm:
        lax.fori_loop(0, nblk, far_round, 0)
    else:
        for d in range(3, ntm):
            unit_arrive(d)
        send_energy()

    if lend:
        @pl.when(is_helper)
        def _():
            def body(n, carry):
                guest_share(lax.rem(p, share), n)
                return carry

            lax.fori_loop(0, lead, body, 0)
            lax.fori_loop(lead, nblk - 1, held_round, 0)
            for e in range(1, share):
                owner = lax.rem(p - e + npt, npt)
                for j in range(npc):
                    relay(e, j, owner).wait_recv()

                def other(n, carry):
                    guest_share(owner, n)
                    return carry

                lax.fori_loop(0, lead, other, 0)
            offs_copy(outward).wait_recv()
            lax.fori_loop(lead, nblk - 1, guest_block, 0)
            arrive(1, nblk - 1, False)
            guest_block(nblk - 1, 0)
            finish_guest()
            half_block(1 - near, nblk - 1)

    spread(shift_rows(qacc[:, BLK:], offs), num_out, num_in, num_send, num_recv)

    def drain(n, carry):
        for s in range(ntm):
            @pl.when(
                (s <= z) & (z < ntm - 1)
                & (((z != ntm - 2) | (s != ntm - 3)) if lend else True)
            )
            def _():
                for h in range(PIECES):
                    hop(s, n, h, right_sem, 1).wait_send()

            @pl.when((s >= z) & (z > 0) & (((z != 1) | (s != 2)) if lend else True))
            def _():
                for h in range(PIECES):
                    hop(s, n, h, left_sem, -1).wait_send()

        return carry

    lax.fori_loop(0, nblk, drain, 0)
    for s in range(ntm):
        @pl.when((s <= z) & (z < ntm - 1))
        def _():
            unit_hop(s, unit_right, 1).wait_send()

        @pl.when((s >= z) & (z > 0))
        def _():
            unit_hop(s, unit_left, -1).wait_send()

    if lend:
        @pl.when(is_end)
        def _():
            for j in range(npc):
                loan(j, inward).wait_send()
            offs_copy(inward).wait_send()

        @pl.when(is_helper)
        def _():
            for j in range(npc):
                for e in range(1, share):
                    relay(e, j, p).wait_send()

    energy = collect(en_out, en_in, en_send, en_recv)
    numerator = collect(num_out, num_in, num_send, num_recv)
    if lend:
        num_out[0] = numerator

        @pl.when(is_end)
        def _():
            total_in = num_out[0]
            for d in range(nch):
                guest_copy(d, inward).wait_recv()
                total_in = total_in + guest_in[d]
            num_out[0] = total_in

        @pl.when(is_helper)
        def _():
            for d in range(nch):
                guest_copy(d, outward).wait_send()

        numerator = num_out[0]
    out_ref[...] = numerator / jnp.sqrt(energy)


def shards(raw_traces, filter_taps, templates, offsets, channel_mask):
    ntm = lax.axis_size("tmpl")
    nch = lax.axis_size("chan")
    rows, length = raw_traces.shape
    group, tlen, local = templates.shape
    nblk = (length - filter_taps.shape[0] + 1) // BLK
    total = nblk * BLK
    lag = (total - SPAN) // nch
    nun = rows // min(LANE, rows)
    npt = lax.axis_size("parts")
    lend = int(ntm == 4 and rows % LANE == 0 and nblk >= 3)
    share = npt if lend and tlen % npt == 0 and group * tlen % (16 * npt) == 0 else 1
    lead = min(LEAD, nblk - 1) if lend else nblk
    f32, bf16, dma = jnp.float32, jnp.bfloat16, pltpu.SemaphoreType.DMA
    any_spec = pl.BlockSpec(memory_space=pl.ANY)
    vmem_spec = pl.BlockSpec(memory_space=pltpu.VMEM)
    return pl.pallas_call(
        functools.partial(kernel, ntm, nch, npt, lend, share, lead),
        out_shape=jax.ShapeDtypeStruct((group, lag), f32),
        in_specs=[
            any_spec, any_spec, any_spec, any_spec, any_spec,
        ],
        out_specs=vmem_spec,
        scratch_shapes=[
            pltpu.VMEM((1, filter_taps.shape[0]), f32),
            pltpu.SMEM((group,), jnp.int32),
            pltpu.VMEM((rows, length), f32),
            pltpu.VMEM((1, 2 * LANE), f32),
            pltpu.VMEM((group, tlen, local), bf16),
            pltpu.VMEM((group, local), jnp.int32),
            pltpu.VMEM((group * tlen, LANE), f32),
            pltpu.VMEM((group * tlen, local), bf16),
            pltpu.VMEM((nblk, local, BLK), bf16),
            pltpu.VMEM((group * tlen, BLK), f32),
            pltpu.VMEM((group, BLK + total), f32),
            pltpu.VMEM((ntm, nun, total), f32),
            pltpu.VMEM((nch, group, lag), f32),
            pltpu.VMEM((nch, group, lag), f32),
            pltpu.VMEM((nch, group, lag), f32),
            pltpu.VMEM((nch, group, lag), f32),
            pltpu.VMEM((group * tlen, rows if lend else LANE), bf16),
            pltpu.VMEM((share, group, BLK + total), f32),
            pltpu.VMEM((nch, group, lag), f32),
            pltpu.VMEM((nch, group, lag), f32),
            pltpu.VMEM((group, LANE), jnp.int32),
            pltpu.VMEM((group, LANE), jnp.int32),
            dma((4,)),
            dma((nblk,)),
            dma((ntm, nblk * PIECES)),
            dma((ntm, nblk * PIECES)),
            dma((ntm, nblk * PIECES)),
            dma((ntm,)),
            dma((ntm,)),
            dma((ntm,)),
            dma((nch,)),
            dma((nch,)),
            dma((nch,)),
            dma((nch,)),
            dma((len(LOANS),)),
            dma((len(LOANS),)),
            dma((npt, len(LOANS))),
            dma((npt, len(LOANS))),
            dma((2,)),
            dma((nch,)),
            dma((nch,)),
        ],
        compiler_params=pltpu.CompilerParams(
            collective_id=0, has_side_effects=True, vmem_limit_bytes=60 * 1024 * 1024
        ),
    )(raw_traces, filter_taps.reshape(1, -1), templates, channel_mask, offsets)


def solution(mesh):
    placed = (
        P(("chan", "tmpl"), "parts"),
        P(),
        P("tmpl", None, "chan"),
        P("tmpl"),
        P("tmpl", None),
    )
    return jax.shard_map(
        shards, mesh=mesh, in_specs=placed, out_specs=P("tmpl", ("parts", "chan")), check_vma=False
    )
```

```python
import functools

import jax
import jax.numpy as jnp
from jax import lax
from jax.experimental import pallas as pl
from jax.experimental.pallas import tpu as pltpu
from jax.sharding import PartitionSpec as P

SPAN = 256
BLK = 256
LANE = 128
MESH = pl.DeviceIdType.MESH
PIECES = 1
LEAD = 3
LOANS = (16, 16, 15, 14, 13, 11, 9, 6)


def left(x, count):
    size = x.shape[-1]
    count = count % size
    return x if count == 0 else pltpu.roll(x, size - count, x.ndim - 1)


def kernel(
    ntm, nch, npt, lend, share, lead, raw_hbm, taps_hbm, tmpl_hbm, mask_hbm, offs_hbm, out_ref,
    taps_ref, offs_ref, raw, tap_row, tmpl, mask, skewed, shaped, rall, prod, qacc, units, num_out, en_out,
    num_in, en_in, guest, gacc, guest_out, guest_in, own_offs, guest_offs,
    load_sem, raw_sem, recv_sem, right_sem, left_sem,
    unit_right, unit_left, unit_recv, num_send, num_recv, en_send, en_recv,
    loan_send, loan_recv, relay_send, relay_recv, offs_sem, guest_send, guest_recv,
):
    z = lax.axis_index("tmpl")
    c = lax.axis_index("chan")
    p = lax.axis_index("parts")
    rows = raw.shape[0]
    group, tlen, local = tmpl.shape
    nblk = rall.shape[0]
    total = nblk * BLK
    unit = min(LANE, rows)
    nun = rows // unit
    side = ntm // 2 if ntm % 2 == 0 and (ntm // 2 * rows) % LANE == 0 else ntm
    width = side * rows
    near = lax.div(z, side)
    is_end = (z == 0) | (z == ntm - 1)
    is_helper = (z == 1) | (z == ntm - 2)
    inward = jnp.where(z == 0, 1, ntm - 2)
    outward = jnp.where(z == 1, 0, ntm - 1)
    lent = jnp.where(z < ntm - 2, 2, ntm - 3) if ntm != 4 else jnp.where(z < 2, 2, 1)

    def load_raw(n, first):
        at = pl.ds(0, BLK + LANE) if first else pl.ds(pl.multiple_of(n * BLK + LANE, LANE), BLK)
        return pltpu.make_async_copy(raw_hbm.at[:, at], raw.at[:, at], raw_sem.at[n])

    load_taps = pltpu.make_async_copy(taps_hbm, taps_ref, load_sem.at[2])
    load_taps.start()
    for n in range(nblk):
        load_raw(n, n == 0).start()
    loads = [
        pltpu.make_async_copy(tmpl_hbm, tmpl, load_sem.at[0]),
        pltpu.make_async_copy(
            mask_hbm.at[:, pl.ds(pl.multiple_of(c * local, LANE), local)], mask, load_sem.at[1]
        ),
        pltpu.make_async_copy(offs_hbm, offs_ref, load_sem.at[3]),
    ]
    for item in loads:
        item.start()

    barrier = pltpu.get_barrier_semaphore()
    @pl.when(z < ntm - 1)
    def _():
        pl.semaphore_signal(
            barrier, inc=1, device_id={"tmpl": lax.rem(z + 1, ntm)}, device_id_type=MESH
        )

    @pl.when(z > 0)
    def _():
        pl.semaphore_signal(
            barrier, inc=1, device_id={"tmpl": lax.rem(z - 1 + ntm, ntm)}, device_id_type=MESH
        )

    for d in range(1, nch):
        pl.semaphore_signal(
            barrier, inc=1, device_id={"chan": lax.rem(c + d, nch)}, device_id_type=MESH
        )

    if lend:
        @pl.when(is_end)
        def _():
            for d in range(1, nch):
                pl.semaphore_signal(
                    barrier, inc=1,
                    device_id={"chan": lax.rem(c + d, nch), "tmpl": inward}, device_id_type=MESH,
                )

        for e in range(1, share):
            pl.semaphore_signal(
                barrier, inc=1, device_id={"parts": lax.rem(p + e, npt)}, device_id_type=MESH
            )

    tap_row[...] = jnp.zeros_like(tap_row)
    load_taps.wait()
    tap_row[:, : taps_ref.shape[1]] = taps_ref[...]
    band = pltpu.roll(
        jnp.broadcast_to(tap_row[...], (LANE, 2 * LANE)), 0, 1, stride=1, stride_axis=0
    )
    band_hi = band.astype(jnp.bfloat16)
    band_lo = (band - band_hi.astype(jnp.float32)).astype(jnp.bfloat16)
    qacc[...] = jnp.zeros_like(qacc)
    if lend:
        @pl.when(is_end)
        def _():
            at = pl.ds(pl.multiple_of(lent * rows, rows), rows)
            for n in range(nblk):
                rall[n, at, :] = jnp.zeros((rows, BLK), jnp.bfloat16)

        @pl.when(is_helper)
        def _():
            gacc[...] = jnp.zeros_like(gacc)

    load_raw(0, True).wait()

    def chunk(src, n):
        return rall.at[n, pl.ds(pl.multiple_of(src * rows, rows), rows), :]

    def hop(src, n, h, sems, step):
        height = rows // PIECES
        at = pl.ds(pl.multiple_of(src * rows + h * height, height), height)
        return pltpu.make_async_remote_copy(
            src_ref=rall.at[n, at, :],
            dst_ref=rall.at[n, at, :],
            send_sem=sems.at[src, n * PIECES + h],
            recv_sem=recv_sem.at[src, n * PIECES + h],
            device_id={"tmpl": lax.rem(z + step + ntm, ntm)},
            device_id_type=MESH,
        )

    def contract(a, b):
        return lax.dot_general(
            a, b, (((1,), (1,)), ((), ())), preferred_element_type=jnp.float32
        )

    def fir(n, carry):
        x = raw[:, pl.ds(pl.multiple_of(n * BLK, BLK), BLK + LANE)]
        hi = x.astype(jnp.bfloat16)
        lo = (x - hi.astype(jnp.float32)).astype(jnp.bfloat16)
        for half in range(BLK // LANE):
            a = hi[:, half * LANE : half * LANE + 2 * LANE]
            b = lo[:, half * LANE : half * LANE + 2 * LANE]
            y = contract(a, band_hi) + (contract(b, band_hi) + contract(a, band_lo))
            y = y.astype(jnp.bfloat16)
            rall[
                n, pl.ds(pl.multiple_of(z * rows, rows), rows), half * LANE : half * LANE + LANE
            ] = y
            y = y.astype(jnp.float32)
            y = y * y
            at = pl.ds(pl.multiple_of(n * BLK + half * LANE, LANE), LANE)
            for u in range(nun):
                units[z, u : u + 1, at] = jnp.sum(
                    y[u * unit : (u + 1) * unit], axis=0, keepdims=True
                )

        return carry

    def send_right(src, n):
        for h in range(PIECES):
            hop(src, n, h, right_sem, 1).start()

    def send_left(src, n):
        for h in range(PIECES):
            hop(src, n, h, left_sem, -1).start()

    goes_right = z < ntm - 1
    goes_left = z > 0
    held_right = (z == 1) & (lead < nblk)
    held_left = (z == ntm - 2) & (lead < nblk)

    def send_own(n, carry):
        @pl.when(goes_right & ((n < lead) | jnp.logical_not(held_right)))
        def _():
            send_right(z, n)

        @pl.when(goes_left & ((n < lead) | jnp.logical_not(held_left)))
        def _():
            send_left(z, n)

        return carry

    def send_held(n, carry):
        @pl.when(held_right)
        def _():
            send_right(z, n)

        @pl.when(held_left)
        def _():
            send_left(z, n)

        return carry

    def fir_next(n, carry):
        load_raw(n, False).wait()
        return fir(n, carry)

    def unit_hop(src, sems, step):
        return pltpu.make_async_remote_copy(
            src_ref=units.at[src],
            dst_ref=units.at[src],
            send_sem=sems.at[src],
            recv_sem=unit_recv.at[src],
            device_id={"tmpl": lax.rem(z + step + ntm, ntm)},
            device_id_type=MESH,
        )

    fir(0, 0)
    pl.semaphore_wait(
        barrier,
        jnp.where(z < ntm - 1, 1, 0) + jnp.where(z > 0, 1, 0) + (nch - 1)
        + (jnp.where(is_helper, nch - 1, 0) + (share - 1) if lend else 0),
    )
    send_own(0, 0)
    lax.fori_loop(1, nblk, fir_next, 0)

    @pl.when(z < ntm - 1)
    def _():
        unit_hop(z, unit_right, 1).start()

    @pl.when(z > 0)
    def _():
        unit_hop(z, unit_left, -1).start()

    lax.fori_loop(1, nblk, send_own, 0)
    for item in loads:
        item.wait()

    def shape_cols(i, carry):
        cols = pl.ds(pl.multiple_of(i * LANE, LANE), LANE)
        flags = mask[:, cols].astype(jnp.float32)
        for k in range(group):
            v = tmpl[k, :, cols].astype(jnp.float32)
            power = jnp.mean(v * v, axis=0, keepdims=True)
            scale = flags[k : k + 1, :] / jnp.sqrt(power + 1e-06)
            skewed[pl.ds(k, tlen, stride=group), :] = v * scale
        shaped[:, cols] = skewed[...].astype(jnp.bfloat16)
        return carry

    lines = tlen * group // share
    npc = len(LOANS)
    cuts = [lines // 16 * sum(LOANS[:j]) // sum(LOANS) * 16 for j in range(npc)] + [lines]

    def loan_lines(owner, j):
        return pl.ds(pl.multiple_of(owner * lines + cuts[j], 16), cuts[j + 1] - cuts[j])

    def loan(j, peer):
        owner = lax.rem(p, share)
        at = loan_lines(owner, j)
        return pltpu.make_async_remote_copy(
            src_ref=shaped.at[at, pl.ds(pl.multiple_of(lent * rows, rows), rows)],
            dst_ref=guest.at[at, :],
            send_sem=loan_send.at[j],
            recv_sem=loan_recv.at[j],
            device_id={"tmpl": peer},
            device_id_type=MESH,
        )

    def relay(e, j, owner):
        at = loan_lines(owner, j)
        return pltpu.make_async_remote_copy(
            src_ref=guest.at[at, :],
            dst_ref=guest.at[at, :],
            send_sem=relay_send.at[e, j],
            recv_sem=relay_recv.at[e, j],
            device_id={"parts": lax.rem(p + e, npt)},
            device_id_type=MESH,
        )

    def offs_copy(peer):
        return pltpu.make_async_remote_copy(
            src_ref=own_offs,
            dst_ref=guest_offs,
            send_sem=offs_sem.at[0],
            recv_sem=offs_sem.at[1],
            device_id={"tmpl": peer},
            device_id_type=MESH,
        )

    offs = jnp.zeros((group, 1), jnp.int32)
    index = lax.broadcasted_iota(jnp.int32, (group, 1), 0)
    for k in range(group):
        offs = jnp.where(index == k, offs_ref[k], offs)

    per = width // LANE
    ahead = rows // LANE if lend else 0
    if lend:
        first = jnp.where(is_end, lent * ahead, near * per)
        lax.fori_loop(first, first + ahead, shape_cols, 0)
        own_offs[...] = jnp.broadcast_to(offs, own_offs.shape)

    if lend:
        @pl.when(is_end)
        def _():
            for j in range(npc):
                loan(j, inward).start()
            offs_copy(inward).start()

    lax.fori_loop(near * per + jnp.where(is_end, 0, ahead), near * per + per, shape_cols, 0)

    def shape_rest():
        first = (1 - near) * per

        def body(i, carry):
            if lend:
                skip = is_end & (lax.div(i, rows // LANE) == lent)

                @pl.when(jnp.logical_not(skip))
                def _():
                    shape_cols(i, 0)
            else:
                shape_cols(i, 0)
            return carry

        lax.fori_loop(first, first + per, body, 0)

    def shift_rows(x, by):
        amount = jnp.broadcast_to(by, x.shape)
        bit = 1
        while bit < SPAN - tlen + 1:
            x = jnp.where((amount & bit) != 0, left(x, bit), x)
            bit *= 2
        return x

    def spread(x, own_ref, in_ref, send, recv):
        lag = own_ref.shape[2]
        for j in range(nch):
            own_ref[j] = x[:, j * lag : (j + 1) * lag]
        for d in range(1, nch):
            other = lax.rem(c + d, nch)
            pltpu.make_async_remote_copy(
                src_ref=own_ref.at[other],
                dst_ref=in_ref.at[d],
                send_sem=send.at[d],
                recv_sem=recv.at[d],
                device_id={"chan": other},
                device_id_type=MESH,
            ).start()

    def collect(own_ref, in_ref, send, recv):
        value = own_ref[c]
        for d in range(1, nch):
            pltpu.make_async_remote_copy(
                src_ref=own_ref.at[lax.rem(c + d, nch)],
                dst_ref=in_ref.at[d],
                send_sem=send.at[d],
                recv_sem=recv.at[d],
                device_id={"chan": lax.rem(c + d, nch)},
                device_id_type=MESH,
            ).wait()
            value = value + in_ref[d]
        return value

    def unit_arrive(d):
        @pl.when(z - d >= 0)
        def _():
            src = lax.rem(z - d + ntm, ntm)
            unit_hop(src, unit_right, 1).wait_recv()

            @pl.when(z < ntm - 1)
            def _():
                unit_hop(src, unit_right, 1).start()

        @pl.when(z + d < ntm)
        def _():
            src = lax.rem(z + d, ntm)
            unit_hop(src, unit_left, -1).wait_recv()

            @pl.when(z > 0)
            def _():
                unit_hop(src, unit_left, -1).start()

    def send_energy():
        masses = jnp.zeros((group, total), jnp.float32)
        for s in range(ntm):
            for u in range(nun):
                at = s * rows + u * unit
                flag = mask[:, at : at + 1].astype(jnp.float32)
                masses = masses + flag * units[s, u : u + 1, :]
        window, width, place, energy = masses, 1, 0, None
        while width <= tlen:
            if tlen & width:
                piece = left(window, place)
                energy = piece if energy is None else energy + piece
                place += width
            window = window + left(window, width)
            width *= 2
        spread(shift_rows(energy, offs), en_out, en_in, en_send, en_recv)

    def arrive(d, n, same):
        def fits(src):
            return (lax.div(src, side) == near) == same

        @pl.when(
            (z - d >= 0) & fits(lax.rem(z - d + ntm, ntm))
            & ((z < ntm - 1) if lend and d == 2 else True)
        )
        def _():
            src = lax.rem(z - d + ntm, ntm)
            for h in range(PIECES):
                hop(src, n, h, right_sem, 1).wait_recv()

                @pl.when(z < ntm - 1 - (1 if lend and d == 1 else 0))
                def _():
                    hop(src, n, h, right_sem, 1).start()

        @pl.when(
            (z + d < ntm) & fits(lax.rem(z + d, ntm)) & ((z > 0) if lend and d == 2 else True)
        )
        def _():
            src = lax.rem(z + d, ntm)
            for h in range(PIECES):
                hop(src, n, h, left_sem, -1).wait_recv()

                @pl.when(z > (1 if lend and d == 1 else 0))
                def _():
                    hop(src, n, h, left_sem, -1).start()

    def arrive_far(n):
        for d in range(2, ntm):
            arrive(d, n, False)

    def skew(n, weights, samples, acc, begin, end):
        prod[: weights.shape[0], :] = jnp.dot(
            weights, samples, preferred_element_type=jnp.float32
        )
        blank = jnp.zeros((group, LANE), jnp.float32)
        span = end - begin
        reach = BLK + (2 * LANE if span > LANE else LANE)
        total_acc = jnp.zeros((group, reach), jnp.float32)

        def row(tap):
            if tap < begin or tap >= end:
                return None
            line = (tap - begin) * group
            return prod[line : line + group, :]

        for g in range(min(LANE, span)):
            low, high = row(g), row(g + LANE)
            if low is None and high is None:
                continue
            carry_in, first, second = blank, blank, blank
            if low is not None:
                first, second = low[:, :LANE], low[:, LANE:]
            if high is not None:
                carry_in = high[:, :LANE]
                first = high[:, LANE:] if low is None else first + high[:, LANE:]
            if span > LANE:
                wide = jnp.concatenate([blank, carry_in, first, second], axis=1)
            else:
                wide = jnp.concatenate([blank, first, second], axis=1)
            total_acc = total_acc + left(wide, g)
        at = pl.ds(pl.multiple_of(n * BLK + 2 * BLK - reach, LANE), reach)
        acc[:, at] = acc[:, at] + total_acc

    def half_block(which, n):
        at = pl.ds(pl.multiple_of(which * width, width), width)
        skew(n, shaped[:, at], rall[n, at, :], qacc, 0, tlen)

    def guest_block(n, carry):
        skew(n, guest[...], chunk(lent, n)[...], gacc.at[0], 0, tlen)
        return carry

    def guest_share(owner, n):
        at = pl.ds(pl.multiple_of(owner * lines, 16), lines)
        skew(n, guest[at, :], chunk(lent, n)[...], gacc.at[owner], 0, tlen // share)

    def guest_copy(d, peer):
        other = lax.rem(c + d, nch)
        return pltpu.make_async_remote_copy(
            src_ref=guest_out.at[other],
            dst_ref=guest_in.at[d],
            send_sem=guest_send.at[d],
            recv_sem=guest_recv.at[d],
            device_id={"chan": other, "tmpl": peer},
            device_id_type=MESH,
        )

    def near_round(n, carry):
        for d in range(1, side):
            arrive(d, n, True)

        @pl.when(n == 0)
        def _():
            unit_arrive(1)

        if side < ntm and lead < nblk:
            @pl.when(n >= lead)
            def _():
                arrive_far(n - lead)

        @pl.when(n == nblk - 1)
        def _():
            lax.fori_loop(lead, nblk, send_held, 0)
            if ntm > 2:
                unit_arrive(2)

        half_block(near, n)
        if side < ntm:
            @pl.when(n == 0)
            def _():
                shape_rest()

        return carry

    def far_round(n, carry):
        @pl.when(n < lead)
        def _():
            arrive(1, n, False)

        @pl.when(n >= (nblk - lead if lead < nblk else 0))
        def _():
            arrive_far(n)

        @pl.when(n == min(2, nblk - 1))
        def _():
            for d in range(3, ntm):
                unit_arrive(d)
            send_energy()

        @pl.when((n < lead) | jnp.logical_not(is_helper))
        def _():
            half_block(1 - near, n)

        if lend:
            for j in range(npc):
                @pl.when(is_helper & (n == min(nblk - 1, 1 + (2 * j + 1) * 6 // (5 * npc))))
                def _():
                    loan(j, outward).wait_recv()
                    for e in range(1, share):
                        relay(e, j, p).start()

        return carry

    def held_round(n, carry):
        arrive(1, n, False)
        half_block(1 - near, n)
        return carry

    def finish_guest():
        moved = gacc[0, :, BLK:]
        if share > 1:
            for q in range(1, share):
                moved = moved + left(gacc[q], q * tlen // share)[:, BLK:]
        moved = shift_rows(moved, guest_offs[:, :1])
        lag = guest_out.shape[2]
        for j in range(nch):
            guest_out[j] = moved[:, j * lag : (j + 1) * lag]
        for d in range(nch):
            guest_copy(d, outward).start()

    lax.fori_loop(0, nblk, near_round, 0)
    if side < ntm:
        lax.fori_loop(0, nblk, far_round, 0)
    else:
        for d in range(3, ntm):
            unit_arrive(d)
        send_energy()

    if lend:
        @pl.when(is_helper)
        def _():
            def body(n, carry):
                guest_share(lax.rem(p, share), n)
                return carry

            lax.fori_loop(0, lead, body, 0)
            def held_share(n, carry):
                arrive(1, n, False)
                guest_share(lax.rem(p, share), n)
                return carry

            lax.fori_loop(lead, nblk - 1, held_share, 0)
            for e in range(1, share):
                owner = lax.rem(p - e + npt, npt)
                for j in range(npc):
                    relay(e, j, owner).wait_recv()

                def other(n, carry):
                    guest_share(owner, n)
                    return carry

                lax.fori_loop(0, nblk - 1, other, 0)
            offs_copy(outward).wait_recv()

            def held_guest(n, carry):
                arrive(1, n, False)
                guest_block(n, 0)
                return carry

            def held_own(n, carry):
                half_block(1 - near, n)
                return carry

            held_guest(nblk - 1, 0)
            finish_guest()
            lax.fori_loop(lead, nblk, held_own, 0)

    spread(shift_rows(qacc[:, BLK:], offs), num_out, num_in, num_send, num_recv)

    def drain(n, carry):
        for s in range(ntm):
            @pl.when(
                (s <= z) & (z < ntm - 1)
                & (((z != ntm - 2) | (s != ntm - 3)) if lend else True)
            )
            def _():
                for h in range(PIECES):
                    hop(s, n, h, right_sem, 1).wait_send()

            @pl.when((s >= z) & (z > 0) & (((z != 1) | (s != 2)) if lend else True))
            def _():
                for h in range(PIECES):
                    hop(s, n, h, left_sem, -1).wait_send()

        return carry

    lax.fori_loop(0, nblk, drain, 0)
    for s in range(ntm):
        @pl.when((s <= z) & (z < ntm - 1))
        def _():
            unit_hop(s, unit_right, 1).wait_send()

        @pl.when((s >= z) & (z > 0))
        def _():
            unit_hop(s, unit_left, -1).wait_send()

    if lend:
        @pl.when(is_end)
        def _():
            for j in range(npc):
                loan(j, inward).wait_send()
            offs_copy(inward).wait_send()

        @pl.when(is_helper)
        def _():
            for j in range(npc):
                for e in range(1, share):
                    relay(e, j, p).wait_send()

    energy = collect(en_out, en_in, en_send, en_recv)
    numerator = collect(num_out, num_in, num_send, num_recv)
    if lend:
        num_out[0] = numerator

        @pl.when(is_end)
        def _():
            total_in = num_out[0]
            for d in range(nch):
                guest_copy(d, inward).wait_recv()
                total_in = total_in + guest_in[d]
            num_out[0] = total_in

        @pl.when(is_helper)
        def _():
            for d in range(nch):
                guest_copy(d, outward).wait_send()

        numerator = num_out[0]
    out_ref[...] = numerator / jnp.sqrt(energy)


def shards(raw_traces, filter_taps, templates, offsets, channel_mask):
    ntm = lax.axis_size("tmpl")
    nch = lax.axis_size("chan")
    rows, length = raw_traces.shape
    group, tlen, local = templates.shape
    nblk = (length - filter_taps.shape[0] + 1) // BLK
    total = nblk * BLK
    lag = (total - SPAN) // nch
    nun = rows // min(LANE, rows)
    npt = lax.axis_size("parts")
    lend = int(ntm == 4 and rows % LANE == 0 and nblk >= 3)
    share = npt if lend and tlen % npt == 0 and group * tlen % (16 * npt) == 0 else 1
    lead = min(LEAD, nblk - 1) if lend else nblk
    f32, bf16, dma = jnp.float32, jnp.bfloat16, pltpu.SemaphoreType.DMA
    any_spec = pl.BlockSpec(memory_space=pl.ANY)
    vmem_spec = pl.BlockSpec(memory_space=pltpu.VMEM)
    return pl.pallas_call(
        functools.partial(kernel, ntm, nch, npt, lend, share, lead),
        out_shape=pltpu.VMEM((group, lag), f32),
        in_specs=[
            any_spec, any_spec, any_spec, any_spec, any_spec,
        ],
        out_specs=vmem_spec,
        scratch_shapes=[
            pltpu.VMEM((1, filter_taps.shape[0]), f32),
            pltpu.SMEM((group,), jnp.int32),
            pltpu.VMEM((rows, length), f32),
            pltpu.VMEM((1, 2 * LANE), f32),
            pltpu.VMEM((group, tlen, local), bf16),
            pltpu.VMEM((group, local), jnp.int32),
            pltpu.VMEM((group * tlen, LANE), f32),
            pltpu.VMEM((group * tlen, local), bf16),
            pltpu.VMEM((nblk, local, BLK), bf16),
            pltpu.VMEM((group * tlen, BLK), f32),
            pltpu.VMEM((group, BLK + total), f32),
            pltpu.VMEM((ntm, nun, total), f32),
            pltpu.VMEM((nch, group, lag), f32),
            pltpu.VMEM((nch, group, lag), f32),
            pltpu.VMEM((nch, group, lag), f32),
            pltpu.VMEM((nch, group, lag), f32),
            pltpu.VMEM((group * tlen, rows if lend else LANE), bf16),
            pltpu.VMEM((share, group, BLK + total), f32),
            pltpu.VMEM((nch, group, lag), f32),
            pltpu.VMEM((nch, group, lag), f32),
            pltpu.VMEM((group, LANE), jnp.int32),
            pltpu.VMEM((group, LANE), jnp.int32),
            dma((4,)),
            dma((nblk,)),
            dma((ntm, nblk * PIECES)),
            dma((ntm, nblk * PIECES)),
            dma((ntm, nblk * PIECES)),
            dma((ntm,)),
            dma((ntm,)),
            dma((ntm,)),
            dma((nch,)),
            dma((nch,)),
            dma((nch,)),
            dma((nch,)),
            dma((len(LOANS),)),
            dma((len(LOANS),)),
            dma((npt, len(LOANS))),
            dma((npt, len(LOANS))),
            dma((2,)),
            dma((nch,)),
            dma((nch,)),
        ],
        compiler_params=pltpu.CompilerParams(
            collective_id=0, has_side_effects=True, vmem_limit_bytes=60 * 1024 * 1024
        ),
    )(raw_traces, filter_taps.reshape(1, -1), templates, channel_mask, offsets)


def solution(mesh):
    placed = (
        P(("chan", "tmpl"), "parts"),
        P(),
        P("tmpl", None, "chan"),
        P("tmpl"),
        P("tmpl", None),
    )
    return jax.shard_map(
        shards, mesh=mesh, in_specs=placed, out_specs=P("tmpl", ("parts", "chan")), check_vma=False
    )
```

```python
import functools

import jax
import jax.numpy as jnp
from jax import lax
from jax.experimental import pallas as pl
from jax.experimental.pallas import tpu as pltpu
from jax.sharding import PartitionSpec as P

SPAN = 256
BLK = 256
LANE = 128
MESH = pl.DeviceIdType.MESH
PIECES = 1
LEAD = 3
LOANS = (16, 16, 15, 14, 13, 11, 9, 6)


def left(x, count):
    size = x.shape[-1]
    count = count % size
    return x if count == 0 else pltpu.roll(x, size - count, x.ndim - 1)


def kernel(
    ntm, nch, npt, lend, share, lead, raw_hbm, taps_hbm, tmpl_hbm, mask_hbm, offs_hbm, out_ref,
    taps_ref, offs_ref, raw, tap_row, tmpl, mask, skewed, shaped, rall, prod, qacc, units, num_out, en_out,
    num_in, en_in, guest, gacc, guest_out, guest_in, own_offs, guest_offs,
    load_sem, raw_sem, recv_sem, right_sem, left_sem,
    unit_right, unit_left, unit_recv, num_send, num_recv, en_send, en_recv,
    loan_send, loan_recv, relay_send, relay_recv, offs_sem, guest_send, guest_recv,
):
    z = lax.axis_index("tmpl")
    c = lax.axis_index("chan")
    p = lax.axis_index("parts")
    rows = raw.shape[0]
    group, tlen, local = tmpl.shape
    nblk = rall.shape[0]
    total = nblk * BLK
    unit = min(LANE, rows)
    nun = rows // unit
    side = ntm // 2 if ntm % 2 == 0 and (ntm // 2 * rows) % LANE == 0 else ntm
    width = side * rows
    near = lax.div(z, side)
    is_end = (z == 0) | (z == ntm - 1)
    is_helper = (z == 1) | (z == ntm - 2)
    inward = jnp.where(z == 0, 1, ntm - 2)
    outward = jnp.where(z == 1, 0, ntm - 1)
    lent = jnp.where(z < ntm - 2, 2, ntm - 3) if ntm != 4 else jnp.where(z < 2, 2, 1)

    def load_raw(n, first):
        at = pl.ds(0, BLK + LANE) if first else pl.ds(pl.multiple_of(n * BLK + LANE, LANE), BLK)
        return pltpu.make_async_copy(raw_hbm.at[:, at], raw.at[:, at], raw_sem.at[n])

    load_taps = pltpu.make_async_copy(taps_hbm, taps_ref, load_sem.at[2])
    load_taps.start()
    for n in range(nblk):
        load_raw(n, n == 0).start()
    loads = [
        pltpu.make_async_copy(tmpl_hbm, tmpl, load_sem.at[0]),
        pltpu.make_async_copy(
            mask_hbm.at[:, pl.ds(pl.multiple_of(c * local, LANE), local)], mask, load_sem.at[1]
        ),
        pltpu.make_async_copy(offs_hbm, offs_ref, load_sem.at[3]),
    ]
    for item in loads:
        item.start()

    barrier = pltpu.get_barrier_semaphore()
    @pl.when(z < ntm - 1)
    def _():
        pl.semaphore_signal(
            barrier, inc=1, device_id={"tmpl": lax.rem(z + 1, ntm)}, device_id_type=MESH
        )

    @pl.when(z > 0)
    def _():
        pl.semaphore_signal(
            barrier, inc=1, device_id={"tmpl": lax.rem(z - 1 + ntm, ntm)}, device_id_type=MESH
        )

    for d in range(1, nch):
        pl.semaphore_signal(
            barrier, inc=1, device_id={"chan": lax.rem(c + d, nch)}, device_id_type=MESH
        )

    if lend:
        @pl.when(is_end)
        def _():
            for d in range(1, nch):
                pl.semaphore_signal(
                    barrier, inc=1,
                    device_id={"chan": lax.rem(c + d, nch), "tmpl": inward}, device_id_type=MESH,
                )

        for e in range(1, share):
            pl.semaphore_signal(
                barrier, inc=1, device_id={"parts": lax.rem(p + e, npt)}, device_id_type=MESH
            )

    tap_row[...] = jnp.zeros_like(tap_row)
    load_taps.wait()
    tap_row[:, : taps_ref.shape[1]] = taps_ref[...]
    band = pltpu.roll(
        jnp.broadcast_to(tap_row[...], (LANE, 2 * LANE)), 0, 1, stride=1, stride_axis=0
    )
    band_hi = band.astype(jnp.bfloat16)
    band_lo = (band - band_hi.astype(jnp.float32)).astype(jnp.bfloat16)
    qacc[...] = jnp.zeros_like(qacc)
    if lend:
        @pl.when(is_end)
        def _():
            at = pl.ds(pl.multiple_of(lent * rows, rows), rows)
            for n in range(nblk):
                rall[n, at, :] = jnp.zeros((rows, BLK), jnp.bfloat16)

        @pl.when(is_helper)
        def _():
            gacc[...] = jnp.zeros_like(gacc)

    load_raw(0, True).wait()

    def chunk(src, n):
        return rall.at[n, pl.ds(pl.multiple_of(src * rows, rows), rows), :]

    def hop(src, n, h, sems, step):
        height = rows // PIECES
        at = pl.ds(pl.multiple_of(src * rows + h * height, height), height)
        return pltpu.make_async_remote_copy(
            src_ref=rall.at[n, at, :],
            dst_ref=rall.at[n, at, :],
            send_sem=sems.at[src, n * PIECES + h],
            recv_sem=recv_sem.at[src, n * PIECES + h],
            device_id={"tmpl": lax.rem(z + step + ntm, ntm)},
            device_id_type=MESH,
        )

    def contract(a, b):
        return lax.dot_general(
            a, b, (((1,), (1,)), ((), ())), preferred_element_type=jnp.float32
        )

    def fir(n, carry):
        x = raw[:, pl.ds(pl.multiple_of(n * BLK, BLK), BLK + LANE)]
        hi = x.astype(jnp.bfloat16)
        lo = (x - hi.astype(jnp.float32)).astype(jnp.bfloat16)
        for half in range(BLK // LANE):
            a = hi[:, half * LANE : half * LANE + 2 * LANE]
            b = lo[:, half * LANE : half * LANE + 2 * LANE]
            y = contract(a, band_hi) + (contract(b, band_hi) + contract(a, band_lo))
            y = y.astype(jnp.bfloat16)
            rall[
                n, pl.ds(pl.multiple_of(z * rows, rows), rows), half * LANE : half * LANE + LANE
            ] = y
            y = y.astype(jnp.float32)
            y = y * y
            at = pl.ds(pl.multiple_of(n * BLK + half * LANE, LANE), LANE)
            for u in range(nun):
                units[z, u : u + 1, at] = jnp.sum(
                    y[u * unit : (u + 1) * unit], axis=0, keepdims=True
                )

        return carry

    def send_right(src, n):
        for h in range(PIECES):
            hop(src, n, h, right_sem, 1).start()

    def send_left(src, n):
        for h in range(PIECES):
            hop(src, n, h, left_sem, -1).start()

    goes_right = z < ntm - 1
    goes_left = z > 0
    held_right = (z == 1) & (lead < nblk)
    held_left = (z == ntm - 2) & (lead < nblk)

    def send_own(n, carry):
        @pl.when(goes_right & ((n < lead) | jnp.logical_not(held_right)))
        def _():
            send_right(z, n)

        @pl.when(goes_left & ((n < lead) | jnp.logical_not(held_left)))
        def _():
            send_left(z, n)

        return carry

    def send_held(n, carry):
        @pl.when(held_right)
        def _():
            send_right(z, n)

        @pl.when(held_left)
        def _():
            send_left(z, n)

        return carry

    def fir_next(n, carry):
        load_raw(n, False).wait()
        return fir(n, carry)

    def unit_hop(src, sems, step):
        return pltpu.make_async_remote_copy(
            src_ref=units.at[src],
            dst_ref=units.at[src],
            send_sem=sems.at[src],
            recv_sem=unit_recv.at[src],
            device_id={"tmpl": lax.rem(z + step + ntm, ntm)},
            device_id_type=MESH,
        )

    fir(0, 0)
    pl.semaphore_wait(
        barrier,
        jnp.where(z < ntm - 1, 1, 0) + jnp.where(z > 0, 1, 0) + (nch - 1)
        + (jnp.where(is_helper, nch - 1, 0) + (share - 1) if lend else 0),
    )
    send_own(0, 0)
    lax.fori_loop(1, nblk, fir_next, 0)

    @pl.when(z < ntm - 1)
    def _():
        unit_hop(z, unit_right, 1).start()

    @pl.when(z > 0)
    def _():
        unit_hop(z, unit_left, -1).start()

    lax.fori_loop(1, nblk, send_own, 0)
    for item in loads:
        item.wait()

    def shape_cols(i, carry):
        cols = pl.ds(pl.multiple_of(i * LANE, LANE), LANE)
        flags = mask[:, cols].astype(jnp.float32)
        for k in range(group):
            v = tmpl[k, :, cols].astype(jnp.float32)
            power = jnp.mean(v * v, axis=0, keepdims=True)
            scale = flags[k : k + 1, :] / jnp.sqrt(power + 1e-06)
            skewed[pl.ds(k, tlen, stride=group), :] = v * scale
        shaped[:, cols] = skewed[...].astype(jnp.bfloat16)
        return carry

    lines = tlen * group // share
    npc = len(LOANS)
    cuts = [lines // 16 * sum(LOANS[:j]) // sum(LOANS) * 16 for j in range(npc)] + [lines]

    def loan_lines(owner, j):
        return pl.ds(pl.multiple_of(owner * lines + cuts[j], 16), cuts[j + 1] - cuts[j])

    def loan(j, peer):
        owner = lax.rem(p, share)
        at = loan_lines(owner, j)
        return pltpu.make_async_remote_copy(
            src_ref=shaped.at[at, pl.ds(pl.multiple_of(lent * rows, rows), rows)],
            dst_ref=guest.at[at, :],
            send_sem=loan_send.at[j],
            recv_sem=loan_recv.at[j],
            device_id={"tmpl": peer},
            device_id_type=MESH,
        )

    def relay(e, j, owner):
        at = loan_lines(owner, j)
        return pltpu.make_async_remote_copy(
            src_ref=guest.at[at, :],
            dst_ref=guest.at[at, :],
            send_sem=relay_send.at[e, j],
            recv_sem=relay_recv.at[e, j],
            device_id={"parts": lax.rem(p + e, npt)},
            device_id_type=MESH,
        )

    def offs_copy(peer):
        return pltpu.make_async_remote_copy(
            src_ref=own_offs,
            dst_ref=guest_offs,
            send_sem=offs_sem.at[0],
            recv_sem=offs_sem.at[1],
            device_id={"tmpl": peer},
            device_id_type=MESH,
        )

    offs = jnp.zeros((group, 1), jnp.int32)
    index = lax.broadcasted_iota(jnp.int32, (group, 1), 0)
    for k in range(group):
        offs = jnp.where(index == k, offs_ref[k], offs)

    per = width // LANE
    ahead = rows // LANE if lend else 0
    if lend:
        first = jnp.where(is_end, lent * ahead, near * per)
        lax.fori_loop(first, first + ahead, shape_cols, 0)
        own_offs[...] = jnp.broadcast_to(offs, own_offs.shape)

    if lend:
        @pl.when(is_end)
        def _():
            for j in range(npc):
                loan(j, inward).start()
            offs_copy(inward).start()

    lax.fori_loop(near * per + jnp.where(is_end, 0, ahead), near * per + per, shape_cols, 0)

    def shape_rest():
        first = (1 - near) * per

        def body(i, carry):
            if lend:
                skip = is_end & (lax.div(i, rows // LANE) == lent)

                @pl.when(jnp.logical_not(skip))
                def _():
                    shape_cols(i, 0)
            else:
                shape_cols(i, 0)
            return carry

        lax.fori_loop(first, first + per, body, 0)

    def shift_rows(x, by):
        amount = jnp.broadcast_to(by, x.shape)
        bit = 1
        while bit < SPAN - tlen + 1:
            digit = (amount // bit) & 3
            y = x
            for step in range(1, 4):
                if step * bit <= SPAN - tlen:
                    y = jnp.where(digit == step, left(x, step * bit), y)
            x = y
            bit *= 4
        return x

    def spread(x, own_ref, in_ref, send, recv):
        lag = own_ref.shape[2]
        for j in range(nch):
            own_ref[j] = x[:, j * lag : (j + 1) * lag]
        for d in range(1, nch):
            other = lax.rem(c + d, nch)
            pltpu.make_async_remote_copy(
                src_ref=own_ref.at[other],
                dst_ref=in_ref.at[d],
                send_sem=send.at[d],
                recv_sem=recv.at[d],
                device_id={"chan": other},
                device_id_type=MESH,
            ).start()

    def collect(own_ref, in_ref, send, recv):
        value = own_ref[c]
        for d in range(1, nch):
            pltpu.make_async_remote_copy(
                src_ref=own_ref.at[lax.rem(c + d, nch)],
                dst_ref=in_ref.at[d],
                send_sem=send.at[d],
                recv_sem=recv.at[d],
                device_id={"chan": lax.rem(c + d, nch)},
                device_id_type=MESH,
            ).wait()
            value = value + in_ref[d]
        return value

    def unit_arrive(d):
        @pl.when(z - d >= 0)
        def _():
            src = lax.rem(z - d + ntm, ntm)
            unit_hop(src, unit_right, 1).wait_recv()

            @pl.when(z < ntm - 1)
            def _():
                unit_hop(src, unit_right, 1).start()

        @pl.when(z + d < ntm)
        def _():
            src = lax.rem(z + d, ntm)
            unit_hop(src, unit_left, -1).wait_recv()

            @pl.when(z > 0)
            def _():
                unit_hop(src, unit_left, -1).start()

    def send_energy():
        masses = jnp.zeros((group, total), jnp.float32)
        for s in range(ntm):
            for u in range(nun):
                at = s * rows + u * unit
                flag = mask[:, at : at + 1].astype(jnp.float32)
                masses = masses + flag * units[s, u : u + 1, :]
        window, width, place, energy = masses, 1, 0, None
        while width <= tlen:
            if tlen & width:
                piece = left(window, place)
                energy = piece if energy is None else energy + piece
                place += width
            window = window + left(window, width)
            width *= 2
        spread(shift_rows(energy, offs), en_out, en_in, en_send, en_recv)

    def arrive(d, n, same):
        def fits(src):
            return (lax.div(src, side) == near) == same

        @pl.when(
            (z - d >= 0) & fits(lax.rem(z - d + ntm, ntm))
            & ((z < ntm - 1) if lend and d == 2 else True)
        )
        def _():
            src = lax.rem(z - d + ntm, ntm)
            for h in range(PIECES):
                hop(src, n, h, right_sem, 1).wait_recv()

                @pl.when(z < ntm - 1 - (1 if lend and d == 1 else 0))
                def _():
                    hop(src, n, h, right_sem, 1).start()

        @pl.when(
            (z + d < ntm) & fits(lax.rem(z + d, ntm)) & ((z > 0) if lend and d == 2 else True)
        )
        def _():
            src = lax.rem(z + d, ntm)
            for h in range(PIECES):
                hop(src, n, h, left_sem, -1).wait_recv()

                @pl.when(z > (1 if lend and d == 1 else 0))
                def _():
                    hop(src, n, h, left_sem, -1).start()

    def arrive_far(n):
        for d in range(2, ntm):
            arrive(d, n, False)

    def skew(n, weights, samples, acc, begin, end):
        prod[: weights.shape[0], :] = jnp.dot(
            weights, samples, preferred_element_type=jnp.float32
        )
        blank = jnp.zeros((group, LANE), jnp.float32)
        span = end - begin
        reach = BLK + (2 * LANE if span > LANE else LANE)
        total_acc = jnp.zeros((group, reach), jnp.float32)

        def row(tap):
            if tap < begin or tap >= end:
                return None
            line = (tap - begin) * group
            return prod[line : line + group, :]

        for g in range(min(LANE, span)):
            low, high = row(g), row(g + LANE)
            if low is None and high is None:
                continue
            carry_in, first, second = blank, blank, blank
            if low is not None:
                first, second = low[:, :LANE], low[:, LANE:]
            if high is not None:
                carry_in = high[:, :LANE]
                first = high[:, LANE:] if low is None else first + high[:, LANE:]
            if span > LANE:
                wide = jnp.concatenate([blank, carry_in, first, second], axis=1)
            else:
                wide = jnp.concatenate([blank, first, second], axis=1)
            total_acc = total_acc + left(wide, g)
        at = pl.ds(pl.multiple_of(n * BLK + 2 * BLK - reach, LANE), reach)
        acc[:, at] = acc[:, at] + total_acc

    def half_block(which, n):
        at = pl.ds(pl.multiple_of(which * width, width), width)
        skew(n, shaped[:, at], rall[n, at, :], qacc, 0, tlen)

    def guest_block(n, carry):
        skew(n, guest[...], chunk(lent, n)[...], gacc.at[0], 0, tlen)
        return carry

    def guest_share(owner, n):
        at = pl.ds(pl.multiple_of(owner * lines, 16), lines)
        skew(n, guest[at, :], chunk(lent, n)[...], gacc.at[owner], 0, tlen // share)

    def guest_copy(d, peer):
        other = lax.rem(c + d, nch)
        return pltpu.make_async_remote_copy(
            src_ref=guest_out.at[other],
            dst_ref=guest_in.at[d],
            send_sem=guest_send.at[d],
            recv_sem=guest_recv.at[d],
            device_id={"chan": other, "tmpl": peer},
            device_id_type=MESH,
        )

    def near_round(n, carry):
        for d in range(1, side):
            arrive(d, n, True)

        @pl.when(n == 0)
        def _():
            unit_arrive(1)

        if side < ntm and lead < nblk:
            @pl.when(n >= lead)
            def _():
                arrive_far(n - lead)

        @pl.when(n == nblk - 1)
        def _():
            lax.fori_loop(lead, nblk, send_held, 0)
            if ntm > 2:
                unit_arrive(2)

        half_block(near, n)
        if side < ntm:
            @pl.when(n == 0)
            def _():
                shape_rest()

        return carry

    def far_round(n, carry):
        @pl.when(n < lead)
        def _():
            arrive(1, n, False)

        @pl.when(n >= (nblk - lead if lead < nblk else 0))
        def _():
            arrive_far(n)

        @pl.when(n == min(2, nblk - 1))
        def _():
            for d in range(3, ntm):
                unit_arrive(d)
            send_energy()

        @pl.when((n < lead) | jnp.logical_not(is_helper))
        def _():
            half_block(1 - near, n)

        if lend:
            for j in range(npc):
                @pl.when(is_helper & (n == min(nblk - 1, 1 + (2 * j + 1) * 6 // (5 * npc))))
                def _():
                    loan(j, outward).wait_recv()
                    for e in range(1, share):
                        relay(e, j, p).start()

        return carry

    def held_round(n, carry):
        arrive(1, n, False)
        half_block(1 - near, n)
        return carry

    def finish_guest():
        moved = gacc[0, :, BLK:]
        if share > 1:
            for q in range(1, share):
                moved = moved + left(gacc[q], q * tlen // share)[:, BLK:]
        moved = shift_rows(moved, guest_offs[:, :1])
        lag = guest_out.shape[2]
        for j in range(nch):
            guest_out[j] = moved[:, j * lag : (j + 1) * lag]
        for d in range(nch):
            guest_copy(d, outward).start()

    lax.fori_loop(0, nblk, near_round, 0)
    if side < ntm:
        lax.fori_loop(0, nblk, far_round, 0)
    else:
        for d in range(3, ntm):
            unit_arrive(d)
        send_energy()

    if lend:
        @pl.when(is_helper)
        def _():
            def body(n, carry):
                guest_share(lax.rem(p, share), n)
                return carry

            lax.fori_loop(0, lead, body, 0)
            def held_share(n, carry):
                arrive(1, n, False)
                guest_share(lax.rem(p, share), n)
                return carry

            lax.fori_loop(lead, nblk - 1, held_share, 0)
            for e in range(1, share):
                owner = lax.rem(p - e + npt, npt)
                for j in range(npc):
                    relay(e, j, owner).wait_recv()

                def other(n, carry):
                    guest_share(owner, n)
                    return carry

                lax.fori_loop(0, nblk - 1, other, 0)
            offs_copy(outward).wait_recv()

            def held_guest(n, carry):
                arrive(1, n, False)
                guest_block(n, 0)
                return carry

            def held_own(n, carry):
                half_block(1 - near, n)
                return carry

            held_guest(nblk - 1, 0)
            finish_guest()
            lax.fori_loop(lead, nblk, held_own, 0)

    spread(shift_rows(qacc[:, BLK:], offs), num_out, num_in, num_send, num_recv)

    def drain(n, carry):
        for s in range(ntm):
            @pl.when(
                (s <= z) & (z < ntm - 1)
                & (((z != ntm - 2) | (s != ntm - 3)) if lend else True)
            )
            def _():
                for h in range(PIECES):
                    hop(s, n, h, right_sem, 1).wait_send()

            @pl.when((s >= z) & (z > 0) & (((z != 1) | (s != 2)) if lend else True))
            def _():
                for h in range(PIECES):
                    hop(s, n, h, left_sem, -1).wait_send()

        return carry

    lax.fori_loop(0, nblk, drain, 0)
    for s in range(ntm):
        @pl.when((s <= z) & (z < ntm - 1))
        def _():
            unit_hop(s, unit_right, 1).wait_send()

        @pl.when((s >= z) & (z > 0))
        def _():
            unit_hop(s, unit_left, -1).wait_send()

    if lend:
        @pl.when(is_end)
        def _():
            for j in range(npc):
                loan(j, inward).wait_send()
            offs_copy(inward).wait_send()

        @pl.when(is_helper)
        def _():
            for j in range(npc):
                for e in range(1, share):
                    relay(e, j, p).wait_send()

    energy = collect(en_out, en_in, en_send, en_recv)
    numerator = collect(num_out, num_in, num_send, num_recv)
    if lend:
        num_out[0] = numerator

        @pl.when(is_end)
        def _():
            total_in = num_out[0]
            for d in range(nch):
                guest_copy(d, inward).wait_recv()
                total_in = total_in + guest_in[d]
            num_out[0] = total_in

        @pl.when(is_helper)
        def _():
            for d in range(nch):
                guest_copy(d, outward).wait_send()

        numerator = num_out[0]
    out_ref[...] = numerator / jnp.sqrt(energy)


def shards(raw_traces, filter_taps, templates, offsets, channel_mask):
    ntm = lax.axis_size("tmpl")
    nch = lax.axis_size("chan")
    rows, length = raw_traces.shape
    group, tlen, local = templates.shape
    nblk = (length - filter_taps.shape[0] + 1) // BLK
    total = nblk * BLK
    lag = (total - SPAN) // nch
    nun = rows // min(LANE, rows)
    npt = lax.axis_size("parts")
    lend = int(ntm == 4 and rows % LANE == 0 and nblk >= 3)
    share = npt if lend and tlen % npt == 0 and group * tlen % (16 * npt) == 0 else 1
    lead = min(LEAD, nblk - 1) if lend else nblk
    f32, bf16, dma = jnp.float32, jnp.bfloat16, pltpu.SemaphoreType.DMA
    any_spec = pl.BlockSpec(memory_space=pl.ANY)
    vmem_spec = pl.BlockSpec(memory_space=pltpu.VMEM)
    return pl.pallas_call(
        functools.partial(kernel, ntm, nch, npt, lend, share, lead),
        out_shape=pltpu.VMEM((group, lag), f32),
        in_specs=[
            any_spec, any_spec, any_spec, any_spec, any_spec,
        ],
        out_specs=vmem_spec,
        scratch_shapes=[
            pltpu.VMEM((1, filter_taps.shape[0]), f32),
            pltpu.SMEM((group,), jnp.int32),
            pltpu.VMEM((rows, length), f32),
            pltpu.VMEM((1, 2 * LANE), f32),
            pltpu.VMEM((group, tlen, local), bf16),
            pltpu.VMEM((group, local), jnp.int32),
            pltpu.VMEM((group * tlen, LANE), f32),
            pltpu.VMEM((group * tlen, local), bf16),
            pltpu.VMEM((nblk, local, BLK), bf16),
            pltpu.VMEM((group * tlen, BLK), f32),
            pltpu.VMEM((group, BLK + total), f32),
            pltpu.VMEM((ntm, nun, total), f32),
            pltpu.VMEM((nch, group, lag), f32),
            pltpu.VMEM((nch, group, lag), f32),
            pltpu.VMEM((nch, group, lag), f32),
            pltpu.VMEM((nch, group, lag), f32),
            pltpu.VMEM((group * tlen, rows if lend else LANE), bf16),
            pltpu.VMEM((share, group, BLK + total), f32),
            pltpu.VMEM((nch, group, lag), f32),
            pltpu.VMEM((nch, group, lag), f32),
            pltpu.VMEM((group, LANE), jnp.int32),
            pltpu.VMEM((group, LANE), jnp.int32),
            dma((4,)),
            dma((nblk,)),
            dma((ntm, nblk * PIECES)),
            dma((ntm, nblk * PIECES)),
            dma((ntm, nblk * PIECES)),
            dma((ntm,)),
            dma((ntm,)),
            dma((ntm,)),
            dma((nch,)),
            dma((nch,)),
            dma((nch,)),
            dma((nch,)),
            dma((len(LOANS),)),
            dma((len(LOANS),)),
            dma((npt, len(LOANS))),
            dma((npt, len(LOANS))),
            dma((2,)),
            dma((nch,)),
            dma((nch,)),
        ],
        compiler_params=pltpu.CompilerParams(
            collective_id=0, has_side_effects=True, vmem_limit_bytes=60 * 1024 * 1024
        ),
    )(raw_traces, filter_taps.reshape(1, -1), templates, channel_mask, offsets)


def solution(mesh):
    placed = (
        P(("chan", "tmpl"), "parts"),
        P(),
        P("tmpl", None, "chan"),
        P("tmpl"),
        P("tmpl", None),
    )
    return jax.shard_map(
        shards, mesh=mesh, in_specs=placed, out_specs=P("tmpl", ("parts", "chan")), check_vma=False
    )
```
